256 devices in a mesh: dp: 8 (over z_hi, core), seq: 32 (over z_lo, x, y).
Axes of the slice: x: 4, y: 4, z: 8 (z_hi: 4, z_lo: 2; z = z_hi * 2 + z_lo), core: 2. Of those that a mesh axis runs over, the one named last changes fastest.
Arguments:
- query: bfloat16 [8, 16384, 1536], P('dp', 'seq'), may hold values from -6 to 6
- key: bfloat16 [8, 16384, 1536], P('dp', 'seq'), may hold values from -6 to 6
- value: bfloat16 [8, 16384, 1536], P('dp', 'seq'), may hold values from -6 to 6
- block_weights: bfloat16 [128, 128, 128], P('seq', 'dp'), may hold values from -0.5 to 0.5
- mix_weights: bfloat16 [128, 128, 128], P('seq', 'dp'), may hold values from -1.5 to 1.5
- block_index: int32 [128, 16], replicated, may hold values from 0 to 127, all different within a row
- cotangent: bfloat16 [8, 16384, 1536], P('dp', 'seq'), may hold values from -6 to 6
Outputs:
- output: bfloat16 [8, 16384, 1536], P('dp', 'seq')
- grad_query: bfloat16 [8, 16384, 1536], P('dp', 'seq')
- grad_key: bfloat16 [8, 16384, 1536], P('dp', 'seq')
- grad_value: bfloat16 [8, 16384, 1536], P('dp', 'seq')
- grad_blocks: float32 [128, 128, 128], P('seq', 'dp')
- grad_mix: float32 [128, 128, 128], P('seq', 'dp')
The draws below stay inside these ranges and needn't reach their ends.
Inputs may be any that keep to these rules, and one draw needn't show every extreme that they name: `block_index`: each row names 16 different blocks, and every block is named by some row.
All inputs are finite; a program needn't handle non-finite values.
Results may differ from the reference program's by a relative error of at most 0.0064.
Values may be sent and summed in bfloat16 or wider, within the bound.
No kernel may reach another device: no remote copies, remote signals or barrier semaphores. Data moves between devices by JAX's collectives and lax.ppermute only.
A program may use at most 64 MiB of HBM per device.

```python
import jax
import jax.numpy as jnp
from jax import lax

CHANNEL_WIDTH = 1536
BS = 128
NNZ = 16
BATCH = 8
SEQUENCE_LENGTH = 16384
NB = 128


def level_of(rng, shape, split, smallest, high):
    loudness, own = 1.0, jax.random.fold_in(rng, 6)
    for dim, shards_of in split:
        steps = jnp.exp(jax.random.uniform(jax.random.fold_in(own, dim), (shards_of,), jnp.float32, smallest / len(split), high / len(split)))
        loudness = loudness * jnp.repeat(steps, shape[dim] // shards_of).reshape([-1 if axis == dim else 1 for axis in range(len(shape))])
    return loudness


def picks_of(key, rows, count, top, lift):
    ranking = jax.random.permutation(jax.random.fold_in(key, 1), count)
    pull = ranking
    for power in range(3):
        pull = pull * pull // count
    pull = pull * lift // count
    chance = jax.random.randint(jax.random.fold_in(key, 2), (rows, count), 0, 4096) + pull
    sure = jax.random.permutation(jax.random.fold_in(key, 3), rows)[jnp.arange(count) % rows]
    chance = jnp.where(jnp.arange(rows)[:, None] == sure[None, :], 1 << 14, chance)
    merit = chance * count + jnp.arange(count)
    return lax.top_k(merit.astype(jnp.int32), top)[1].astype(jnp.int32)


def bell_draw(stream_key, shape, spread, most, shards=(), kind=jnp.bfloat16):
    factor_of = level_of(stream_key, shape, shards, -0.22, 0.18) if shards else 1.0
    values = jax.random.normal(stream_key, shape, jnp.float32) * spread * factor_of
    return jnp.minimum(jnp.maximum(values, -most), most).astype(kind)


def setup_inputs(seed: int = 0) -> dict:
    keys = jax.random.split(jax.random.key(seed), 8)
    return {
        "query": bell_draw(keys[0], (BATCH, SEQUENCE_LENGTH, CHANNEL_WIDTH), 1.0, 6.0, ((0, 8), (1, 32))),
        "key": bell_draw(keys[1], (BATCH, SEQUENCE_LENGTH, CHANNEL_WIDTH), 1.0, 6.0, ((0, 8), (1, 32))),
        "value": bell_draw(keys[2], (BATCH, SEQUENCE_LENGTH, CHANNEL_WIDTH), 1.0, 6.0, ((0, 8), (1, 32))),
        "block_weights": bell_draw(keys[3], (NB, BS, BS), BS ** -0.5, 0.5, ((0, 32), (1, 8))),
        "mix_weights": bell_draw(keys[4], (BS, NB, NB), NNZ ** -0.5, 1.5, ((0, 32), (1, 8))),
        "block_index": picks_of(keys[5], NB, NB, NNZ, 0),
        "cotangent": bell_draw(keys[6], (BATCH, SEQUENCE_LENGTH, CHANNEL_WIDTH), 1.0, 6.0, ((0, 8), (1, 32))),
    }


def rounded_value(values):
    return lax.optimization_barrier(values.astype(jnp.bfloat16)).astype(jnp.float32)


def block_mask(block_index):
    columns = jnp.arange(NB, dtype=jnp.int32)
    hits = (block_index[:, :, None] == columns[None, None, :]).astype(jnp.float32)
    return jnp.max(hits, axis=1)


def reference(query, key, value, block_weights, mix_weights, block_index, cotangent):
    pattern = block_mask(block_index)
    masked = mix_weights.astype(jnp.float32) * pattern[None]
    block_tiles = block_weights.astype(jnp.float32)

    def sample(items):
        query_row, key_row, value_row, cot_row = items
        query_f = query_row.astype(jnp.float32)
        key_f = key_row.astype(jnp.float32)
        value_f = value_row.astype(jnp.float32)
        cot_f = cot_row.astype(jnp.float32)
        split_parts = rounded_value(key_f * value_f).reshape(NB, BS, CHANNEL_WIDTH)
        first_factor = rounded_value(jnp.einsum("nfq,nql->nfl", block_tiles, split_parts))
        mixed = rounded_value(jnp.einsum("jik,kjd->ijd", masked, first_factor)).reshape(SEQUENCE_LENGTH, CHANNEL_WIDTH)
        output = (query_f * mixed).astype(jnp.bfloat16)
        grad_query = (cot_f * mixed).astype(jnp.bfloat16)
        grad_mixed = rounded_value(cot_f * query_f).reshape(NB, BS, CHANNEL_WIDTH)
        first_factor_gradient = rounded_value(jnp.einsum("jik,ijd->kjd", masked, grad_mixed))
        mix_term = jnp.einsum("ijd,kjd->jik", grad_mixed, first_factor) * pattern[None]
        product_gradient = jnp.einsum("obj,obv->ojv", block_tiles, first_factor_gradient).reshape(SEQUENCE_LENGTH, CHANNEL_WIDTH)
        grad_key = (product_gradient * value_f).astype(jnp.bfloat16)
        grad_value = (product_gradient * key_f).astype(jnp.bfloat16)
        sparse_block_part = jnp.einsum("ejo,eso->ejs", first_factor_gradient, split_parts)
        return output, grad_query, grad_key, grad_value, sparse_block_part, mix_term

    results = lax.map(sample, (query, key, value, cotangent))
    return (results[0], results[1], results[2], results[3],
            jnp.sum(results[4], axis=0), jnp.sum(results[5], axis=0))
```

```python
import jax
import jax.numpy as jnp
from jax import lax
from jax.experimental import pallas as pl
from jax.experimental.pallas import tpu as pltpu
from jax.sharding import PartitionSpec as P

BF16 = jnp.bfloat16
F32 = jnp.float32
VMEM_LIMIT = 48 * 1024 * 1024


def dot(a, b, ca=1, cb=0):
    return lax.dot_general(a, b, (((ca,), (cb,)), ((), ())), preferred_element_type=F32)


def one_hot(size, column_of):
    rows = lax.broadcasted_iota(jnp.int32, (size, size), 0)
    columns = lax.broadcasted_iota(jnp.int32, (size, size), 1)
    return (columns == column_of(rows)).astype(F32).astype(BF16)


def slab_order(r):
    return ((r >> 2) & 3) * 64 + (r >> 4) * 4 + (r & 3)


def offset_order(r):
    return (r & 63) * 4 + (r >> 6)


def to_slabs(perm, x):
    halves = []
    for g in range(2):
        part = jnp.concatenate([x[k * 128 + g * 64 : k * 128 + g * 64 + 64] for k in range(4)], axis=0)
        halves.append(dot(perm, part).astype(BF16))
    return jnp.concatenate(halves, axis=0)


def from_slabs(perm, x):
    halves = [dot(perm, x[g * 256 : g * 256 + 256], ca=0).astype(BF16) for g in range(2)]
    return [jnp.concatenate([h[k * 64 : k * 64 + 64] for h in halves], axis=0) for k in range(4)]


def by_offset(perm, x):
    halves = [dot(perm, x[g * 256 : g * 256 + 256]).astype(BF16) for g in range(2)]
    return [jnp.concatenate([h[j * 64 : j * 64 + 64] for h in halves], axis=0) for j in range(4)]


def times(a, b):
    return (a.astype(F32) * b.astype(F32)).astype(BF16)


def call(kernel, name, grid, in_specs, out_specs, out_shape, scratch=(), flops=0, nbytes=0, aliases=None):
    return pl.pallas_call(
        kernel,
        name=name,
        grid=grid,
        in_specs=in_specs,
        out_specs=out_specs,
        out_shape=out_shape,
        scratch_shapes=list(scratch),
        input_output_aliases=aliases or {},
        cost_estimate=pl.CostEstimate(flops=flops, transcendentals=0, bytes_accessed=nbytes),
        compiler_params=pltpu.CompilerParams(
            vmem_limit_bytes=VMEM_LIMIT, dimension_semantics=("arbitrary",) * len(grid)
        ),
    )


def rows_spec(width):
    return pl.BlockSpec((512, width), lambda d: (0, d))


def slab_spec(width, half=0):
    return pl.BlockSpec((32, 16, width), lambda d: (0, half, d))


def whole(*shape):
    return pl.BlockSpec(shape, lambda *g: (0,) * len(shape))


def gate_kernel(q_ref, c_ref, o_ref, perm):
    @pl.when(pl.program_id(0) == 0)
    def _():
        perm[...] = one_hot(256, slab_order)

    o_ref[...] = to_slabs(perm[...], times(q_ref[...], c_ref[...])).reshape(o_ref.shape)


def first_kernel(w_ref, k_ref, v_ref, o_ref, perm, blocks):
    @pl.when(pl.program_id(0) == 0)
    def _():
        perm[...] = one_hot(256, slab_order)
        for s in range(8):
            blocks[:, s * 16 : s * 16 + 16, :] = w_ref[s, 0:4]

    product = times(k_ref[...], v_ref[...])
    first = jnp.concatenate(
        [dot(blocks[k], product[k * 128 : k * 128 + 128]).astype(BF16) for k in range(4)], axis=0
    )
    o_ref[...] = to_slabs(perm[...], first).reshape(o_ref.shape)


def factor_kernel(w_ref, idx_ref, m_ref, mt_ref, p_ref, diag):
    columns = lax.broadcasted_iota(jnp.int32, (128, 128), 1)
    hits = jnp.zeros((128, 128), F32)
    for n in range(idx_ref.shape[1]):
        hits = jnp.maximum(hits, (idx_ref[:, n : n + 1] == columns).astype(F32))
    p_ref[...] = hits
    diag[...] = jnp.zeros_like(diag)
    for j in range(4):
        mix = jnp.concatenate([w_ref[s, 4 + j] for s in range(8)], axis=0).astype(F32)
        diag[j * 128 : j * 128 + 128, j * 128 : j * 128 + 128] = (mix * hits).astype(BF16)
    spread = one_hot(512, lambda r: (r & 3) * 128 + (r >> 2))
    rows = dot(spread, diag[...]).astype(BF16)
    m_ref[...] = dot(rows, spread, cb=1).astype(BF16)
    rows_t = dot(spread, diag[...], cb=1).astype(BF16)
    mt_ref[...] = dot(rows_t, spread, cb=1).astype(BF16)


def back_kernel(m_ref, x_ref, _, o_ref):
    x = x_ref[...].reshape(512, x_ref.shape[2])
    o_ref[...] = dot(m_ref[...], x).astype(BF16).reshape(o_ref.shape)


def mix_kernel(m_ref, x_ref, o_ref):
    x = x_ref[...].reshape(512, x_ref.shape[2])
    o_ref[...] = dot(m_ref[...], x).astype(BF16).reshape(o_ref.shape)


def grads_kernel(core_ref, w_ref, pat_ref, gm_ref, f_ref, gf_ref, k_ref, v_ref, gk_ref, gv_ref, send_ref, keep_ref,
                 perm, sort, blocks, acc):
    @pl.when(pl.program_id(0) == 0)
    def _():
        perm[...] = one_hot(256, slab_order)
        sort[...] = one_hot(256, offset_order)
        for s in range(8):
            blocks[:, s * 16 : s * 16 + 16, :] = w_ref[s, 0:4]
        acc[...] = jnp.zeros_like(acc)

    width = k_ref.shape[1]
    grad_first = from_slabs(perm[...], gf_ref[...].reshape(512, width))
    for k in range(4):
        rows = slice(k * 128, k * 128 + 128)
        key, value = k_ref[rows, :].astype(F32), v_ref[rows, :].astype(F32)
        acc[k] += dot(grad_first[k], (key * value).astype(BF16), cb=1)
        grad = dot(blocks[k], grad_first[k], ca=0)
        gk_ref[rows, :] = (grad * value).astype(BF16)
        gv_ref[rows, :] = (grad * key).astype(BF16)
    left = by_offset(sort[...], gm_ref[...].reshape(512, width))
    right = by_offset(sort[...], f_ref[...].reshape(512, width))
    for j in range(4):
        acc[4 + j] += dot(left[j], right[j], cb=1)

    @pl.when(pl.program_id(0) == pl.num_programs(0) - 1)
    def _():
        for j in range(4):
            acc[4 + j] = acc[4 + j] * pat_ref[...]
        core = core_ref[0]
        for z in range(4):
            keep_ref[z] = acc[:, pl.ds(pl.multiple_of(z * 32 + core * 16, 16), 16), :]
            send_ref[z] = acc[:, pl.ds(pl.multiple_of(z * 32 + 16 - core * 16, 16), 16), :]


def pair_kernel(z_ref, keep_ref, got_ref, own_ref, *out_refs):
    z = z_ref[0]
    own_ref[...] = keep_ref[z] + got_ref[z]
    for r, out in enumerate(out_refs, start=1):
        t = lax.rem(z + r, 4)
        out[...] = (keep_ref[t] + got_ref[t]).astype(BF16)


def tail_kernel(x_ref, q_ref, c_ref, o_ref, gq_ref, perm):
    @pl.when(pl.program_id(0) == 0)
    def _():
        perm[...] = one_hot(256, slab_order)

    mixed = from_slabs(perm[...], x_ref[...].reshape(512, x_ref.shape[2]))
    for k in range(4):
        rows = slice(k * 128, k * 128 + 128)
        m = mixed[k].astype(F32)
        o_ref[rows, :] = (q_ref[rows, :].astype(F32) * m).astype(BF16)
        gq_ref[rows, :] = (c_ref[rows, :].astype(F32) * m).astype(BF16)


def on_device(query, key, value, block_weights, mix_weights, block_index, cotangent):
    channels = query.shape[2]
    q, k, v, cot = (a.reshape(512, channels) for a in (query, key, value, cotangent))
    width = 256
    grid = (channels // width,)
    rows, slab = rows_spec(width), slab_spec(width)
    smem = pl.BlockSpec(memory_space=pltpu.SMEM)
    row_shape = jax.ShapeDtypeStruct((512, channels), BF16)
    slab_shape = jax.ShapeDtypeStruct((32, 16, channels), BF16)
    pair_shape = jax.ShapeDtypeStruct((32, 32, channels), BF16)
    perm = pltpu.VMEM((256, 256), BF16)
    size = 512 * channels * 2
    work = 2 * 512 * 512 * channels

    def exchange(x):
        return lax.all_to_all(x, "seq", split_axis=0, concat_axis=0, tiled=True)

    place = lax.axis_index("dp")
    core = (place % 2).reshape(1)
    z = (place // 2).reshape(1)

    gated = call(gate_kernel, "gate", grid, [rows, rows], slab, slab_shape, [perm], work // 2, 3 * size)(q, cot)
    grad_cols = exchange(gated)

    weights = lax.all_gather(jnp.concatenate([block_weights, mix_weights], axis=0), "dp", axis=0)
    weights_spec = whole(8, 8, 16, 128)
    out = call(
        first_kernel, "first", grid, [weights_spec, rows, rows], slab, pair_shape,
        [perm, pltpu.VMEM((4, 128, 128), BF16)], work, 3 * size,
    )(weights, k, v)
    factor, factor_t, pattern = call(
        factor_kernel, "factor", (), [weights_spec, whole(128, 16)],
        [whole(512, 512), whole(512, 512), whole(128, 128)],
        [jax.ShapeDtypeStruct((512, 512), BF16), jax.ShapeDtypeStruct((512, 512), BF16), jax.ShapeDtypeStruct((128, 128), F32)],
        [pltpu.VMEM((512, 512), BF16)], work, size,
    )(weights, block_index)
    square = whole(512, 512)
    out = call(
        back_kernel, "back", grid, [square, slab, pl.BlockSpec(memory_space=pl.ANY)],
        slab_spec(width, 1), pair_shape, (), work, 2 * size, {2: 0},
    )(factor_t, grad_cols, out)
    got = exchange(out)
    mixed_cols = call(mix_kernel, "mix", grid, [square, slab], slab, slab_shape, (), work, 2 * size)(factor, got)
    returned = exchange(mixed_cols)

    part = jax.ShapeDtypeStruct((4, 8, 16, 128), F32)
    grad_key, grad_value, send, keep = call(
        grads_kernel, "grads", grid,
        [smem, weights_spec, whole(128, 128), slab, slab, slab_spec(width, 1), rows, rows],
        [rows, rows, whole(4, 8, 16, 128), whole(4, 8, 16, 128)], [row_shape, row_shape, part, part],
        [perm, perm, pltpu.VMEM((4, 128, 128), BF16), pltpu.VMEM((8, 128, 128), F32)], 4 * work, 7 * size,
    )(core, weights, pattern, grad_cols, got, got, k, v)
    swapped = lax.ppermute(send, "dp", [(i, i ^ 1) for i in range(8)])
    shard = jax.ShapeDtypeStruct((8, 16, 128), BF16)
    own, *others = call(
        pair_kernel, "pair", (), [smem, whole(4, 8, 16, 128), whole(4, 8, 16, 128)], [whole(8, 16, 128)] * 4,
        [jax.ShapeDtypeStruct((8, 16, 128), F32), shard, shard, shard],
    )(z, keep, swapped)
    total = own
    for r, other in enumerate(others, start=1):
        hop = [(i, ((i // 2 + r) % 4) * 2 + i % 2) for i in range(8)]
        total = total + lax.ppermute(other, "dp", hop).astype(F32)

    output, grad_query = call(
        tail_kernel, "tail", grid, [slab, rows, rows], [rows, rows], [row_shape, row_shape], [perm], work // 2, 5 * size
    )(returned, q, cot)
    wide = query.shape
    return (
        output.reshape(wide), grad_query.reshape(wide), grad_key.reshape(wide), grad_value.reshape(wide),
        total[0:4], total[4:8],
    )


def solution(mesh):
    placed = (
        P("dp", "seq", None),
        P("dp", "seq", None),
        P("dp", "seq", None),
        P("seq", "dp", None),
        P("seq", "dp", None),
        P(),
        P("dp", "seq", None),
    )
    return jax.shard_map(
        on_device,
        mesh=mesh,
        in_specs=placed,
        out_specs=(
            P("dp", "seq", None),
            P("dp", "seq", None),
            P("dp", "seq", None),
            P("dp", "seq", None),
            P("seq", "dp", None),
            P("seq", "dp", None),
        ),
        check_vma=False,
    )
```

```python
import jax
import jax.numpy as jnp
from jax import lax
from jax.experimental import pallas as pl
from jax.experimental.pallas import tpu as pltpu
from jax.sharding import PartitionSpec as P

BF16 = jnp.bfloat16
F32 = jnp.float32
MIB = 1024 * 1024


def dot(a, b, ca=1, cb=0):
    return lax.dot_general(a, b, (((ca,), (cb,)), ((), ())), preferred_element_type=F32)


def one_hot(size, column_of):
    rows = lax.broadcasted_iota(jnp.int32, (size, size), 0)
    columns = lax.broadcasted_iota(jnp.int32, (size, size), 1)
    return (columns == column_of(rows)).astype(F32).astype(BF16)


def slab_order(r):
    return ((r >> 2) & 3) * 64 + (r >> 4) * 4 + (r & 3)


def offset_order(r):
    return (r & 63) * 4 + (r >> 6)


def to_slabs(perm, x):
    halves = []
    for g in range(2):
        part = jnp.concatenate([x[k * 128 + g * 64 : k * 128 + g * 64 + 64] for k in range(4)], axis=0)
        halves.append(dot(perm, part).astype(BF16))
    return jnp.concatenate(halves, axis=0)


def from_slabs(perm, x):
    halves = [dot(perm, x[g * 256 : g * 256 + 256], ca=0).astype(BF16) for g in range(2)]
    return [jnp.concatenate([h[k * 64 : k * 64 + 64] for h in halves], axis=0) for k in range(4)]


def by_offset(perm, x):
    halves = [dot(perm, x[g * 256 : g * 256 + 256]).astype(BF16) for g in range(2)]
    return [jnp.concatenate([h[j * 64 : j * 64 + 64] for h in halves], axis=0) for j in range(4)]


def times(a, b):
    return (a.astype(F32) * b.astype(F32)).astype(BF16)


def call(kernel, name, grid, in_specs, out_specs, out_shape, scratch=(), flops=0, nbytes=0, aliases=None, vmem=8):
    return pl.pallas_call(
        kernel,
        name=name,
        grid=grid,
        in_specs=in_specs,
        out_specs=out_specs,
        out_shape=out_shape,
        scratch_shapes=list(scratch),
        input_output_aliases=aliases or {},
        cost_estimate=pl.CostEstimate(flops=flops, transcendentals=0, bytes_accessed=nbytes),
        compiler_params=pltpu.CompilerParams(
            vmem_limit_bytes=vmem * MIB, dimension_semantics=("arbitrary",) * len(grid)
        ),
    )


def rows_spec(width):
    return pl.BlockSpec((512, width), lambda d: (0, d))


def slab_spec(width, half=0):
    return pl.BlockSpec((32, 16, width), lambda d: (0, half, d))


def whole(*shape):
    return pl.BlockSpec(shape, lambda *g: (0,) * len(shape))


VMEM_SPEC = pl.BlockSpec(memory_space=pltpu.VMEM)


def gate_kernel(q_ref, c_ref, o_ref, perm):
    @pl.when(pl.program_id(0) == 0)
    def _():
        perm[...] = one_hot(256, slab_order)

    o_ref[...] = to_slabs(perm[...], times(q_ref[...], c_ref[...])).reshape(o_ref.shape)


def first_kernel(blocks, k_ref, v_ref, o_ref, perm):
    @pl.when(pl.program_id(0) == 0)
    def _():
        perm[...] = one_hot(256, slab_order)

    product = times(k_ref[...], v_ref[...])
    first = jnp.concatenate(
        [dot(blocks[k], product[k * 128 : k * 128 + 128]).astype(BF16) for k in range(4)], axis=0
    )
    o_ref[...] = to_slabs(perm[...], first).reshape(o_ref.shape)


def factor_kernel(place_ref, w0_ref, w1_ref, w2_ref, w3_ref, mate_ref, idx_ref, b_ref, m_ref, mt_ref, p_ref, diag, mixes):
    place = place_ref[0]
    core = lax.rem(place, 2)
    for r, w_ref in enumerate((w0_ref, w1_ref, w2_ref, w3_ref)):
        z = lax.rem(lax.div(place, 2) + 4 - r, 4)
        own = pl.ds(pl.multiple_of(z * 32 + core * 16, 16), 16)
        mate = pl.ds(pl.multiple_of(z * 32 + 16 - core * 16, 16), 16)
        b_ref[:, own, :] = w_ref[0:4]
        b_ref[:, mate, :] = mate_ref[r, 0:4]
        mixes[:, own, :] = w_ref[4:8]
        mixes[:, mate, :] = mate_ref[r, 4:8]
    columns = lax.broadcasted_iota(jnp.int32, (128, 128), 1)
    hits = jnp.zeros((128, 128), F32)
    for n in range(idx_ref.shape[1]):
        hits = jnp.maximum(hits, (idx_ref[:, n : n + 1] == columns).astype(F32))
    p_ref[...] = hits
    diag[...] = jnp.zeros_like(diag)
    for j in range(4):
        diag[j * 128 : j * 128 + 128, j * 128 : j * 128 + 128] = (mixes[j].astype(F32) * hits).astype(BF16)
    spread = one_hot(512, lambda r: (r & 3) * 128 + (r >> 2))
    rows = dot(spread, diag[...]).astype(BF16)
    m_ref[...] = dot(rows, spread, cb=1).astype(BF16)
    rows_t = dot(spread, diag[...], cb=1).astype(BF16)
    mt_ref[...] = dot(rows_t, spread, cb=1).astype(BF16)


def back_kernel(m_ref, x_ref, _, o_ref):
    x = x_ref[...].reshape(512, x_ref.shape[2])
    o_ref[...] = dot(m_ref[...], x).astype(BF16).reshape(o_ref.shape)


def mix_kernel(m_ref, x_ref, o_ref):
    x = x_ref[...].reshape(512, x_ref.shape[2])
    o_ref[...] = dot(m_ref[...], x).astype(BF16).reshape(o_ref.shape)


def sums_kernel(core_ref, pat_ref, gm_ref, f_ref, gf_ref, k_ref, v_ref, send_ref, keep_ref, perm, sort, acc):
    @pl.when(pl.program_id(0) == 0)
    def _():
        perm[...] = one_hot(256, slab_order)
        sort[...] = one_hot(256, offset_order)
        acc[...] = jnp.zeros_like(acc)

    width = k_ref.shape[1]
    grad_first = from_slabs(perm[...], gf_ref[...].reshape(512, width))
    product = times(k_ref[...], v_ref[...])
    for k in range(4):
        acc[k] += dot(grad_first[k], product[k * 128 : k * 128 + 128], cb=1)
    left = by_offset(sort[...], gm_ref[...].reshape(512, width))
    right = by_offset(sort[...], f_ref[...].reshape(512, width))
    for j in range(4):
        acc[4 + j] += dot(left[j], right[j], cb=1)

    @pl.when(pl.program_id(0) == pl.num_programs(0) - 1)
    def _():
        for j in range(4):
            acc[4 + j] = acc[4 + j] * pat_ref[...]
        core = core_ref[0]
        for z in range(4):
            keep_ref[z] = acc[:, pl.ds(pl.multiple_of(z * 32 + core * 16, 16), 16), :]
            send_ref[z] = acc[:, pl.ds(pl.multiple_of(z * 32 + 16 - core * 16, 16), 16), :]


def grads_kernel(blocks, gf_ref, k_ref, v_ref, gk_ref, gv_ref, perm):
    @pl.when(pl.program_id(0) == 0)
    def _():
        perm[...] = one_hot(256, slab_order)

    grad_first = from_slabs(perm[...], gf_ref[...].reshape(512, k_ref.shape[1]))
    for k in range(4):
        rows = slice(k * 128, k * 128 + 128)
        grad = dot(blocks[k], grad_first[k], ca=0)
        gk_ref[rows, :] = (grad * v_ref[rows, :].astype(F32)).astype(BF16)
        gv_ref[rows, :] = (grad * k_ref[rows, :].astype(F32)).astype(BF16)


def pair_kernel(z_ref, keep_ref, got_ref, own_ref, *out_refs):
    z = z_ref[0]
    own_ref[...] = keep_ref[z] + got_ref[z]
    for r, out in enumerate(out_refs, start=1):
        t = lax.rem(z + r, 4)
        out[...] = (keep_ref[t] + got_ref[t]).astype(BF16)


def tail_kernel(x_ref, q_ref, c_ref, o_ref, gq_ref, perm):
    @pl.when(pl.program_id(0) == 0)
    def _():
        perm[...] = one_hot(256, slab_order)

    mixed = from_slabs(perm[...], x_ref[...].reshape(512, x_ref.shape[2]))
    for k in range(4):
        rows = slice(k * 128, k * 128 + 128)
        m = mixed[k].astype(F32)
        o_ref[rows, :] = (q_ref[rows, :].astype(F32) * m).astype(BF16)
        gq_ref[rows, :] = (c_ref[rows, :].astype(F32) * m).astype(BF16)


def on_device(query, key, value, block_weights, mix_weights, block_index, cotangent):
    channels = query.shape[2]
    q, k, v, cot = (a.reshape(512, channels) for a in (query, key, value, cotangent))
    width = 256
    grid = (channels // width,)
    rows, slab = rows_spec(width), slab_spec(width)
    smem = pl.BlockSpec(memory_space=pltpu.SMEM)
    row_shape = jax.ShapeDtypeStruct((512, channels), BF16)
    slab_shape = pltpu.HBM((32, 16, channels), BF16)
    pair_shape = pltpu.HBM((32, 32, channels), BF16)
    perm = pltpu.VMEM((256, 256), BF16)
    size = 512 * channels * 2
    work = 2 * 512 * 512 * channels

    def exchange(x):
        return lax.all_to_all(x, "seq", split_axis=0, concat_axis=0, tiled=True)

    place = lax.axis_index("dp").astype(jnp.int32).reshape(1)
    core, z = place & 1, place >> 1

    def pinned(x):
        return pltpu.with_memory_space_constraint(x, pltpu.HBM)

    def held(x):
        return pltpu.with_memory_space_constraint(x, pltpu.VMEM)

    def hop(r):
        return [(i, ((i // 2 + r) % 4) * 2 + i % 2) for i in range(8)]

    mate = [(i, i ^ 1) for i in range(8)]
    gated = call(gate_kernel, "gate", grid, [rows, rows], slab, slab_shape, [perm], work // 2, 3 * size)(
        pinned(q), pinned(cot)
    )
    own_rows = jnp.concatenate([block_weights, mix_weights], axis=0)
    gated, own_rows = lax.optimization_barrier((gated, own_rows))
    grad_cols = pinned(exchange(gated))

    column = [own_rows] + [lax.ppermute(own_rows, "dp", hop(r)) for r in (1, 2, 3)]
    other = lax.ppermute(jnp.stack(column), "dp", mate)
    shard_spec = whole(8, 16, 128)
    blocks, factor, factor_t, pattern = call(
        factor_kernel, "factor", (), [smem] + [shard_spec] * 4 + [whole(4, 8, 16, 128), whole(128, 16)],
        [VMEM_SPEC] * 4,
        [pltpu.VMEM((4, 128, 128), BF16), pltpu.VMEM((512, 512), BF16), pltpu.VMEM((512, 512), BF16),
         pltpu.VMEM((128, 128), F32)],
        [pltpu.VMEM((512, 512), BF16), pltpu.VMEM((4, 128, 128), BF16)], work, size,
    )(place, *column, other, block_index)
    out = call(first_kernel, "first", grid, [VMEM_SPEC, rows, rows], slab, pair_shape, [perm], work, 3 * size)(
        held(blocks), pinned(k), pinned(v)
    )
    out = call(
        back_kernel, "back", grid, [VMEM_SPEC, slab, pl.BlockSpec(memory_space=pl.ANY)],
        slab_spec(width, 1), pair_shape, (), work, 2 * size, {2: 0},
    )(held(factor_t), grad_cols, out)
    got = exchange(out)
    mixed_cols = call(mix_kernel, "mix", grid, [VMEM_SPEC, slab], slab, slab_shape, (), work, 2 * size)(held(factor), got)
    returned = exchange(mixed_cols)

    part = jax.ShapeDtypeStruct((4, 8, 16, 128), F32)
    send, keep = call(
        sums_kernel, "sums", grid,
        [smem, VMEM_SPEC, slab, slab, slab_spec(width, 1), rows, rows],
        [whole(4, 8, 16, 128), whole(4, 8, 16, 128)], [part, part],
        [perm, perm, pltpu.VMEM((8, 128, 128), F32)], 3 * work, 5 * size,
    )(core, held(pattern), grad_cols, got, got, pinned(k), pinned(v))
    grad_key, grad_value = call(
        grads_kernel, "grads", grid, [VMEM_SPEC, slab_spec(width, 1), rows, rows], [rows, rows],
        [row_shape, row_shape], [perm], work, 5 * size,
    )(held(blocks), got, pinned(k), pinned(v))
    swapped = lax.ppermute(send, "dp", mate)
    shard = jax.ShapeDtypeStruct((8, 16, 128), BF16)
    own, *others = call(
        pair_kernel, "pair", (), [smem, whole(4, 8, 16, 128), whole(4, 8, 16, 128)], [whole(8, 16, 128)] * 4,
        [jax.ShapeDtypeStruct((8, 16, 128), F32), shard, shard, shard],
    )(z, keep, swapped)
    total = own
    for r, other in enumerate(others, start=1):
        total = total + lax.ppermute(other, "dp", hop(r)).astype(F32)

    output, grad_query = call(
        tail_kernel, "tail", grid, [slab, rows, rows], [rows, rows], [row_shape, row_shape], [perm], work // 2, 5 * size
    )(returned, pinned(q), pinned(cot))
    wide = query.shape
    return (
        output.reshape(wide), grad_query.reshape(wide), grad_key.reshape(wide), grad_value.reshape(wide),
        total[0:4], total[4:8],
    )


def solution(mesh):
    placed = (
        P("dp", "seq", None),
        P("dp", "seq", None),
        P("dp", "seq", None),
        P("seq", "dp", None),
        P("seq", "dp", None),
        P(),
        P("dp", "seq", None),
    )
    return jax.shard_map(
        on_device,
        mesh=mesh,
        in_specs=placed,
        out_specs=(
            P("dp", "seq", None),
            P("dp", "seq", None),
            P("dp", "seq", None),
            P("dp", "seq", None),
            P("seq", "dp", None),
            P("seq", "dp", None),
        ),
        check_vma=False,
    )
```

```python
import jax
import jax.numpy as jnp
from jax import lax
from jax.experimental import pallas as pl
from jax.experimental.pallas import tpu as pltpu
from jax.sharding import PartitionSpec as P

BF16 = jnp.bfloat16
F32 = jnp.float32
MIB = 1024 * 1024
STEP = 512


def dot(a, b, ca=1, cb=0):
    return lax.dot_general(a, b, (((ca,), (cb,)), ((), ())), preferred_element_type=F32)


def one_hot(size, column_of):
    rows = lax.broadcasted_iota(jnp.int32, (size, size), 0)
    columns = lax.broadcasted_iota(jnp.int32, (size, size), 1)
    return (columns == column_of(rows)).astype(F32).astype(BF16)


def slab_order(r):
    return ((r >> 2) & 3) * 64 + (r >> 4) * 4 + (r & 3)


def offset_order(r):
    return (r & 63) * 4 + (r >> 6)


def to_slabs(perm, x):
    halves = []
    for g in range(2):
        part = jnp.concatenate([x[k * 128 + g * 64 : k * 128 + g * 64 + 64] for k in range(4)], axis=0)
        halves.append(dot(perm, part).astype(BF16))
    return jnp.concatenate(halves, axis=0)


def from_slabs(perm, x):
    halves = [dot(perm, x[g * 256 : g * 256 + 256], ca=0).astype(BF16) for g in range(2)]
    return [jnp.concatenate([h[k * 64 : k * 64 + 64] for h in halves], axis=0) for k in range(4)]


def by_offset(perm, x):
    halves = [dot(perm, x[g * 256 : g * 256 + 256]).astype(BF16) for g in range(2)]
    return [jnp.concatenate([h[j * 64 : j * 64 + 64] for h in halves], axis=0) for j in range(4)]


def times(a, b):
    return (a.astype(F32) * b.astype(F32)).astype(BF16)


def call(kernel, name, grid, in_specs, out_specs, out_shape, scratch=(), flops=0, nbytes=0, aliases=None, vmem=8):
    return pl.pallas_call(
        kernel,
        name=name,
        grid=grid,
        in_specs=in_specs,
        out_specs=out_specs,
        out_shape=out_shape,
        scratch_shapes=list(scratch),
        input_output_aliases=aliases or {},
        cost_estimate=pl.CostEstimate(flops=flops, transcendentals=0, bytes_accessed=nbytes),
        compiler_params=pltpu.CompilerParams(
            vmem_limit_bytes=vmem * MIB, dimension_semantics=("arbitrary",) * len(grid)
        ),
    )


def chunk_of(ref, index, width, rows=0):
    columns = pl.ds(index * width, width)
    if len(ref.shape) == 2:
        return ref.at[:, columns]
    return ref.at[:, pl.ds(rows, 16), columns] if ref.shape[0] == 32 else ref.at[:, :, columns]


def streamed(body, name, ins, out_shapes, width, consts=(), out_rows=0, extra=(), aliases=None, scratch=(), prepare=None,
             flops=0, nbytes=0, vmem=16):
    channels = ins[0].shape[-1]
    count = channels // width
    n_const, n_in, n_extra, n_out = len(consts), len(ins), len(extra), len(out_shapes)

    def buffer(array):
        shape = array.shape
        return pltpu.VMEM((count, *((32, 16) if len(shape) == 3 and shape[0] == 32 else shape[:-1]), width), BF16)

    def kernel(*refs):
        const_refs, refs = refs[:n_const], refs[n_const:]
        in_refs, refs = refs[:n_in], refs[n_in + n_extra :]
        out_refs, refs = refs[:n_out], refs[n_out:]
        bufs, refs = refs[:n_in], refs[n_in:]
        outs, refs = refs[:n_out], refs[n_out:]
        in_sem, out_sem, scratch_refs = refs[0], refs[1], refs[2:]
        arriving, leaving = [], []
        for c in range(count):
            arriving.append([
                pltpu.make_async_copy(chunk_of(in_refs[i], c, width), bufs[i].at[c], in_sem.at[i, c]) for i in range(n_in)
            ])
            for copy in arriving[c]:
                copy.start()
        if prepare is not None:
            prepare(*scratch_refs)
        for c in range(count):
            for copy in arriving[c]:
                copy.wait()
            values = [buf[c].reshape(512, width) for buf in bufs]
            for o, make in enumerate(body(const_refs, scratch_refs, *values)):
                outs[o][c] = make().reshape(outs[o].shape[1:])
                copy = pltpu.make_async_copy(outs[o].at[c], chunk_of(out_refs[o], c, width, out_rows), out_sem.at[o, c])
                copy.start()
                leaving.append(copy)
        for copy in leaving:
            copy.wait()

    return pl.pallas_call(
        kernel,
        name=name,
        in_specs=[VMEM_SPEC] * n_const + [pl.BlockSpec(memory_space=pl.ANY)] * (n_in + n_extra),
        out_specs=[pl.BlockSpec(memory_space=pltpu.HBM)] * n_out,
        out_shape=list(out_shapes),
        scratch_shapes=[buffer(x) for x in ins]
        + [buffer(x) for x in out_shapes]
        + [pltpu.SemaphoreType.DMA((n_in, count)), pltpu.SemaphoreType.DMA((n_out, count))]
        + list(scratch),
        input_output_aliases=aliases or {},
        cost_estimate=pl.CostEstimate(flops=flops, transcendentals=0, bytes_accessed=nbytes),
        compiler_params=pltpu.CompilerParams(vmem_limit_bytes=vmem * MIB),
    )(*[held(x) for x in consts], *ins, *extra)


def pinned(x):
    return pltpu.with_memory_space_constraint(x, pltpu.HBM)


def held(x):
    return pltpu.with_memory_space_constraint(x, pltpu.VMEM)


def rows_spec(width):
    return pl.BlockSpec((512, width), lambda d: (0, d))


def slab_spec(width, half=0):
    return pl.BlockSpec((32, 16, width), lambda d: (0, half, d))


def whole(*shape):
    return pl.BlockSpec(shape, lambda *g: (0,) * len(shape))


VMEM_SPEC = pl.BlockSpec(memory_space=pltpu.VMEM)


def make_slab_order(perm):
    perm[...] = one_hot(256, slab_order)


def make_offset_order(perm):
    perm[...] = one_hot(256, offset_order)


def gate_body(consts, scratch, q, cot):
    return [lambda: to_slabs(scratch[0][...], times(q, cot))]


def factor_body(consts, scratch, x):
    return [lambda: dot(consts[0][...], x).astype(BF16)]


def back_body(consts, scratch, x):
    return [
        lambda: dot(consts[0][...], x).astype(BF16),
        lambda: jnp.concatenate(by_offset(scratch[0][...], x), axis=0),
    ]


def tail_body(consts, scratch, x, q, cot):
    mixed = jnp.concatenate(from_slabs(scratch[0][...], x), axis=0)
    return [lambda: times(q, mixed), lambda: times(cot, mixed)]


def first_kernel(blocks, k_ref, v_ref, o_ref, perm):
    @pl.when(pl.program_id(0) == 0)
    def _():
        perm[...] = one_hot(256, slab_order)

    product = times(k_ref[...], v_ref[...])
    first = jnp.concatenate(
        [dot(blocks[k], product[k * 128 : k * 128 + 128]).astype(BF16) for k in range(4)], axis=0
    )
    o_ref[...] = to_slabs(perm[...], first).reshape(o_ref.shape)


def factor_kernel(place_ref, w0_ref, w1_ref, w2_ref, w3_ref, mate_ref, idx_ref, b_ref, m_ref, mt_ref, p_ref, diag, mixes):
    place = place_ref[0]
    core = lax.rem(place, 2)
    for r, w_ref in enumerate((w0_ref, w1_ref, w2_ref, w3_ref)):
        z = lax.rem(lax.div(place, 2) + 4 - r, 4)
        own = pl.ds(pl.multiple_of(z * 32 + core * 16, 16), 16)
        mate = pl.ds(pl.multiple_of(z * 32 + 16 - core * 16, 16), 16)
        b_ref[:, own, :] = w_ref[0:4]
        b_ref[:, mate, :] = mate_ref[r, 0:4]
        mixes[:, own, :] = w_ref[4:8]
        mixes[:, mate, :] = mate_ref[r, 4:8]
    columns = lax.broadcasted_iota(jnp.int32, (128, 128), 1)
    hits = jnp.zeros((128, 128), F32)
    for n in range(idx_ref.shape[1]):
        hits = jnp.maximum(hits, (idx_ref[:, n : n + 1] == columns).astype(F32))
    p_ref[...] = hits
    diag[...] = jnp.zeros_like(diag)
    for j in range(4):
        diag[j * 128 : j * 128 + 128, j * 128 : j * 128 + 128] = (mixes[j].astype(F32) * hits).astype(BF16)
    spread = one_hot(512, lambda r: (r & 3) * 128 + (r >> 2))
    rows = dot(spread, diag[...]).astype(BF16)
    m_ref[...] = dot(rows, spread, cb=1).astype(BF16)
    rows_t = dot(spread, diag[...], cb=1).astype(BF16)
    mt_ref[...] = dot(rows_t, spread, cb=1).astype(BF16)


def sums_kernel(core_ref, pat_ref, gm_ref, f_ref, gf_ref, k_ref, v_ref, send_ref, keep_ref, perm, sort, acc):
    @pl.when(pl.program_id(0) == 0)
    def _():
        perm[...] = one_hot(256, slab_order)
        sort[...] = one_hot(256, offset_order)
        acc[...] = jnp.zeros_like(acc)

    width = k_ref.shape[1]
    grad_first = from_slabs(perm[...], gf_ref[...].reshape(512, width))
    product = times(k_ref[...], v_ref[...])
    for k in range(4):
        acc[k] += dot(grad_first[k], product[k * 128 : k * 128 + 128], cb=1)
    right = by_offset(sort[...], f_ref[...].reshape(512, width))
    for j in range(4):
        acc[4 + j] += dot(gm_ref[j], right[j], cb=1)

    @pl.when(pl.program_id(0) == pl.num_programs(0) - 1)
    def _():
        for j in range(4):
            acc[4 + j] = acc[4 + j] * pat_ref[...]
        core = core_ref[0]
        for z in range(4):
            keep_ref[z] = acc[:, pl.ds(pl.multiple_of(z * 32 + core * 16, 16), 16), :]
            send_ref[z] = acc[:, pl.ds(pl.multiple_of(z * 32 + 16 - core * 16, 16), 16), :]


def grads_kernel(blocks, gf_ref, k_ref, v_ref, gk_ref, gv_ref, perm):
    @pl.when(pl.program_id(0) == 0)
    def _():
        perm[...] = one_hot(256, slab_order)

    grad_first = from_slabs(perm[...], gf_ref[...].reshape(512, k_ref.shape[1]))
    for k in range(4):
        rows = slice(k * 128, k * 128 + 128)
        grad = dot(blocks[k], grad_first[k], ca=0)
        gk_ref[rows, :] = (grad * v_ref[rows, :].astype(F32)).astype(BF16)
        gv_ref[rows, :] = (grad * k_ref[rows, :].astype(F32)).astype(BF16)


def pair_kernel(z_ref, keep_ref, got_ref, own_ref, *out_refs):
    z = z_ref[0]
    own_ref[...] = keep_ref[z] + got_ref[z]
    for r, out in enumerate(out_refs, start=1):
        t = lax.rem(z + r, 4)
        out[...] = (keep_ref[t] + got_ref[t]).astype(BF16)


def on_device(query, key, value, block_weights, mix_weights, block_index, cotangent):
    channels = query.shape[2]
    q, k, v, cot = (a.reshape(512, channels) for a in (query, key, value, cotangent))
    width = 256
    grid = (channels // width,)
    rows, slab = rows_spec(width), slab_spec(width)
    smem = pl.BlockSpec(memory_space=pltpu.SMEM)
    row_shape = jax.ShapeDtypeStruct((512, channels), BF16)
    pinned_rows = pltpu.HBM((512, channels), BF16)
    slab_shape = pltpu.HBM((32, 16, channels), BF16)
    pair_shape = pltpu.HBM((32, 32, channels), BF16)
    perm = pltpu.VMEM((256, 256), BF16)
    size = 512 * channels * 2
    work = 2 * 512 * 512 * channels

    def exchange(x):
        return lax.all_to_all(x, "seq", split_axis=0, concat_axis=0, tiled=True)

    place = lax.axis_index("dp").astype(jnp.int32).reshape(1)
    core, z = place & 1, place >> 1

    def hop(r):
        return [(i, ((i // 2 + r) % 4) * 2 + i % 2) for i in range(8)]

    mate = [(i, i ^ 1) for i in range(8)]
    own_rows = jnp.concatenate([block_weights, mix_weights], axis=0)
    column = [own_rows] + [lax.ppermute(own_rows, "dp", hop(r)) for r in (1, 2, 3)]
    (gated,) = streamed(
        gate_body, "gate", [pinned(q), pinned(cot)], [slab_shape], STEP, scratch=[perm], prepare=make_slab_order,
        flops=work // 2, nbytes=3 * size,
    )
    gated, *column = lax.optimization_barrier((gated, *column))
    grad_cols = exchange(gated)
    other = lax.ppermute(jnp.stack(column), "dp", mate)
    shard_spec = whole(8, 16, 128)
    blocks, factor, factor_t, pattern = call(
        factor_kernel, "factor", (), [smem] + [shard_spec] * 4 + [whole(4, 8, 16, 128), whole(128, 16)],
        [VMEM_SPEC] * 4,
        [pltpu.VMEM((4, 128, 128), BF16), pltpu.VMEM((512, 512), BF16), pltpu.VMEM((512, 512), BF16),
         pltpu.VMEM((128, 128), F32)],
        [pltpu.VMEM((512, 512), BF16), pltpu.VMEM((4, 128, 128), BF16)], work, size,
    )(place, *column, other, block_index)
    out = call(first_kernel, "first", grid, [VMEM_SPEC, rows, rows], slab, pair_shape, [perm], work, 3 * size)(
        held(blocks), pinned(k), pinned(v)
    )
    out, left = streamed(
        back_body, "back", [grad_cols], [pair_shape, pltpu.HBM((4, 128, channels), BF16)], STEP, consts=[factor_t],
        out_rows=16, extra=[out], aliases={2: 0}, scratch=[perm], prepare=make_offset_order,
        flops=2 * work, nbytes=3 * size,
    )
    got = exchange(out)
    (mixed_cols,) = streamed(factor_body, "mix", [got], [slab_shape], STEP, consts=[factor], flops=work, nbytes=2 * size)
    returned = exchange(mixed_cols)

    part = jax.ShapeDtypeStruct((4, 8, 16, 128), F32)
    send, keep = call(
        sums_kernel, "sums", grid,
        [smem, VMEM_SPEC, pl.BlockSpec((4, 128, width), lambda d: (0, 0, d)), slab, slab_spec(width, 1), rows, rows],
        [whole(4, 8, 16, 128), whole(4, 8, 16, 128)], [part, part],
        [perm, perm, pltpu.VMEM((8, 128, 128), F32)], 3 * work, 5 * size,
    )(core, held(pattern), left, got, got, pinned(k), pinned(v))
    grad_key, grad_value = call(
        grads_kernel, "grads", grid, [VMEM_SPEC, slab_spec(width, 1), rows, rows], [rows, rows],
        [row_shape, row_shape], [perm], work, 5 * size,
    )(held(blocks), got, pinned(k), pinned(v))
    swapped = lax.ppermute(send, "dp", mate)
    shard = jax.ShapeDtypeStruct((8, 16, 128), BF16)
    own, *others = call(
        pair_kernel, "pair", (), [smem, whole(4, 8, 16, 128), whole(4, 8, 16, 128)], [whole(8, 16, 128)] * 4,
        [jax.ShapeDtypeStruct((8, 16, 128), F32), shard, shard, shard],
    )(z, keep, swapped)
    total = own
    for r, other in enumerate(others, start=1):
        total = total + lax.ppermute(other, "dp", hop(r)).astype(F32)

    output, grad_query = streamed(
        tail_body, "tail", [returned, pinned(q), pinned(cot)], [pinned_rows, pinned_rows], STEP,
        scratch=[perm], prepare=make_slab_order, flops=work // 2, nbytes=5 * size,
    )
    wide = query.shape
    return (
        output.reshape(wide), grad_query.reshape(wide), grad_key.reshape(wide), grad_value.reshape(wide),
        total[0:4], total[4:8],
    )


def solution(mesh):
    placed = (
        P("dp", "seq", None),
        P("dp", "seq", None),
        P("dp", "seq", None),
        P("seq", "dp", None),
        P("seq", "dp", None),
        P(),
        P("dp", "seq", None),
    )
    return jax.shard_map(
        on_device,
        mesh=mesh,
        in_specs=placed,
        out_specs=(
            P("dp", "seq", None),
            P("dp", "seq", None),
            P("dp", "seq", None),
            P("dp", "seq", None),
            P("seq", "dp", None),
            P("seq", "dp", None),
        ),
        check_vma=False,
    )
```

```python
import jax
import jax.numpy as jnp
from jax import lax
from jax.experimental import pallas as pl
from jax.experimental.pallas import tpu as pltpu
from jax.sharding import PartitionSpec as P

BF16 = jnp.bfloat16
F32 = jnp.float32
MIB = 1024 * 1024
STEP = 512
WIDE = 512


def dot(a, b, ca=1, cb=0):
    return lax.dot_general(a, b, (((ca,), (cb,)), ((), ())), preferred_element_type=F32)


def one_hot(size, column_of):
    rows = lax.broadcasted_iota(jnp.int32, (size, size), 0)
    columns = lax.broadcasted_iota(jnp.int32, (size, size), 1)
    return (columns == column_of(rows)).astype(F32).astype(BF16)


def slab_order(r):
    return ((r >> 2) & 3) * 64 + (r >> 4) * 4 + (r & 3)


def offset_order(r):
    return (r & 63) * 4 + (r >> 6)


def to_slabs(perm, x):
    halves = []
    for g in range(2):
        part = jnp.concatenate([x[k * 128 + g * 64 : k * 128 + g * 64 + 64] for k in range(4)], axis=0)
        halves.append(dot(perm, part).astype(BF16))
    return jnp.concatenate(halves, axis=0)


def from_slabs(perm, x):
    halves = [dot(perm, x[g * 256 : g * 256 + 256], ca=0).astype(BF16) for g in range(2)]
    return [jnp.concatenate([h[k * 64 : k * 64 + 64] for h in halves], axis=0) for k in range(4)]


def by_offset(perm, x):
    halves = [dot(perm, x[g * 256 : g * 256 + 256]).astype(BF16) for g in range(2)]
    return [jnp.concatenate([h[j * 64 : j * 64 + 64] for h in halves], axis=0) for j in range(4)]


def times(a, b):
    return (a.astype(F32) * b.astype(F32)).astype(BF16)


def call(kernel, name, grid, in_specs, out_specs, out_shape, scratch=(), flops=0, nbytes=0, aliases=None, vmem=12):
    return pl.pallas_call(
        kernel,
        name=name,
        grid=grid,
        in_specs=in_specs,
        out_specs=out_specs,
        out_shape=out_shape,
        scratch_shapes=list(scratch),
        input_output_aliases=aliases or {},
        cost_estimate=pl.CostEstimate(flops=flops, transcendentals=0, bytes_accessed=nbytes),
        compiler_params=pltpu.CompilerParams(
            vmem_limit_bytes=vmem * MIB, dimension_semantics=("arbitrary",) * len(grid)
        ),
    )


def chunk_of(ref, index, width, rows=0):
    columns = pl.ds(index * width, width)
    if len(ref.shape) == 2:
        return ref.at[:, columns]
    return ref.at[:, pl.ds(rows, 16), columns] if ref.shape[0] == 32 else ref.at[:, :, columns]


def streamed(body, name, ins, out_shapes, width, consts=(), resident=None, out_rows=0, extra=(), aliases=None, scratch=(),
             prepare=None, echo=None, flops=0, nbytes=0, vmem=16):
    channels = out_shapes[0].shape[-1]
    count = channels // width
    vmem_in = list(consts) + ([] if resident is None else [resident])
    n_vmem, n_in, n_extra, n_out = len(vmem_in), len(ins), len(extra), len(out_shapes)

    def buffer(array):
        shape = array.shape
        return pltpu.VMEM((count, *((32, 16) if len(shape) == 3 and shape[0] == 32 else shape[:-1]), width), BF16)

    def kernel(*refs):
        vmem_refs, refs = refs[:n_vmem], refs[n_vmem:]
        in_refs, refs = refs[:n_in], refs[n_in + n_extra :]
        out_refs, refs = refs[:n_out], refs[n_out:]
        leaving = []
        if echo is not None:
            leaving.append(pltpu.make_async_copy(vmem_refs[-1], refs[0], refs[-1].at[0]))
            leaving[0].start()
            refs = refs[1:-1]
        bufs, refs = refs[:n_in], refs[n_in:]
        outs, refs = refs[:n_out], refs[n_out:]
        in_sem, out_sem, scratch_refs = refs[0], refs[1], refs[2:]
        arriving = []
        for c in range(count):
            arriving.append([
                pltpu.make_async_copy(chunk_of(in_refs[i], c, width), bufs[i].at[c], in_sem.at[i, c]) for i in range(n_in)
            ])
            for copy in arriving[c]:
                copy.start()
        if prepare is not None:
            prepare(*scratch_refs)
        for c in range(count):
            for copy in arriving[c]:
                copy.wait()
            values = [buf[c].reshape(512, width) for buf in bufs]
            if resident is not None:
                values = [vmem_refs[-1][:, 0:16, c * width : c * width + width].reshape(512, width)] + values
            for o, make in enumerate(body(vmem_refs, scratch_refs, *values)):
                outs[o][c] = make().reshape(outs[o].shape[1:])
                copy = pltpu.make_async_copy(outs[o].at[c], chunk_of(out_refs[o], c, width, out_rows), out_sem.at[o, c])
                copy.start()
                leaving.append(copy)
        for copy in leaving:
            copy.wait()

    return pl.pallas_call(
        kernel,
        name=name,
        in_specs=[VMEM_SPEC] * n_vmem + [pl.BlockSpec(memory_space=pl.ANY)] * (n_in + n_extra),
        out_specs=[pl.BlockSpec(memory_space=pltpu.HBM)] * (n_out + (echo is not None)),
        out_shape=list(out_shapes) + ([] if echo is None else [echo]),
        scratch_shapes=[buffer(x) for x in ins]
        + [buffer(x) for x in out_shapes]
        + [pltpu.SemaphoreType.DMA((max(n_in, 1), count)), pltpu.SemaphoreType.DMA((n_out, count))]
        + list(scratch)
        + ([] if echo is None else [pltpu.SemaphoreType.DMA((1,))]),
        input_output_aliases=aliases or {},
        cost_estimate=pl.CostEstimate(flops=flops, transcendentals=0, bytes_accessed=nbytes),
        compiler_params=pltpu.CompilerParams(vmem_limit_bytes=vmem * MIB),
    )(*[held(x) for x in vmem_in], *ins, *extra)


def pinned(x):
    return pltpu.with_memory_space_constraint(x, pltpu.HBM)


def held(x):
    return pltpu.with_memory_space_constraint(x, pltpu.VMEM)


def rows_spec(width):
    return pl.BlockSpec((512, width), lambda d: (0, d))


def slab_spec(width, half=0):
    return pl.BlockSpec((32, 16, width), lambda d: (0, half, d))


def whole(*shape):
    return pl.BlockSpec(shape, lambda *g: (0,) * len(shape))


VMEM_SPEC = pl.BlockSpec(memory_space=pltpu.VMEM)


def make_slab_order(perm):
    perm[...] = one_hot(256, slab_order)


def gate_body(consts, scratch, q, cot):
    return [lambda: to_slabs(scratch[0][...], times(q, cot))]


def factor_body(consts, scratch, x):
    return [lambda: dot(consts[0][...], x).astype(BF16)]


def tail_body(consts, scratch, x, q, cot):
    mixed = jnp.concatenate(from_slabs(scratch[0][...], x), axis=0)
    return [lambda: times(q, mixed), lambda: times(cot, mixed)]


def pack_kernel(*refs):
    ins, out_ref, sem = refs[:-2], refs[-2], refs[-1]
    copies, start = [], 0
    for i, ref in enumerate(ins):
        copies.append(pltpu.make_async_copy(ref, out_ref.at[pl.ds(start, ref.shape[0])], sem.at[i]))
        start += ref.shape[0]
    for copy in copies:
        copy.start()
    for copy in copies:
        copy.wait()


def pack(name, *arrays):
    shape = (sum(a.shape[0] for a in arrays), *arrays[0].shape[1:])
    return pl.pallas_call(
        pack_kernel,
        name=name,
        in_specs=[pl.BlockSpec(memory_space=pl.ANY)] * len(arrays),
        out_specs=VMEM_SPEC,
        out_shape=pltpu.VMEM(shape, arrays[0].dtype),
        scratch_shapes=[pltpu.SemaphoreType.DMA((len(arrays),))],
        compiler_params=pltpu.CompilerParams(vmem_limit_bytes=4 * MIB),
    )(*[pinned(a) for a in arrays])


def first_kernel(blocks, k_ref, v_ref, o_ref, perm):
    @pl.when(pl.program_id(0) == 0)
    def _():
        perm[...] = one_hot(256, slab_order)

    product = times(k_ref[...], v_ref[...])
    first = jnp.concatenate(
        [dot(blocks[k], product[k * 128 : k * 128 + 128]).astype(BF16) for k in range(4)], axis=0
    )
    o_ref[...] = to_slabs(perm[...], first).reshape(o_ref.shape)


def factor_kernel(place_ref, w0_ref, w1_ref, w2_ref, w3_ref, mate_ref, idx_ref, b_ref, m_ref, mt_ref, p_ref, diag, mixes):
    place = place_ref[0]
    core = lax.rem(place, 2)
    for r, w_ref in enumerate((w0_ref, w1_ref, w2_ref, w3_ref)):
        z = lax.rem(lax.div(place, 2) + 4 - r, 4)
        own = pl.ds(pl.multiple_of(z * 32 + core * 16, 16), 16)
        mate = pl.ds(pl.multiple_of(z * 32 + 16 - core * 16, 16), 16)
        b_ref[:, own, :] = w_ref[0:4]
        b_ref[:, mate, :] = mate_ref[r, 0:4]
        mixes[:, own, :] = w_ref[4:8]
        mixes[:, mate, :] = mate_ref[r, 4:8]
    columns = lax.broadcasted_iota(jnp.int32, (128, 128), 1)
    hits = jnp.zeros((128, 128), F32)
    for n in range(idx_ref.shape[1]):
        hits = jnp.maximum(hits, (idx_ref[:, n : n + 1] == columns).astype(F32))
    p_ref[...] = hits
    diag[...] = jnp.zeros_like(diag)
    for j in range(4):
        diag[j * 128 : j * 128 + 128, j * 128 : j * 128 + 128] = (mixes[j].astype(F32) * hits).astype(BF16)
    spread = one_hot(512, lambda r: (r & 3) * 128 + (r >> 2))
    rows = dot(spread, diag[...]).astype(BF16)
    m_ref[...] = dot(rows, spread, cb=1).astype(BF16)
    rows_t = dot(spread, diag[...], cb=1).astype(BF16)
    mt_ref[...] = dot(rows_t, spread, cb=1).astype(BF16)


def sums_kernel(core_ref, pat_ref, gm_ref, f_ref, gf_ref, k_ref, v_ref, send_ref, keep_ref, perm, sort, acc):
    @pl.when(pl.program_id(0) == 0)
    def _():
        perm[...] = one_hot(256, slab_order)
        sort[...] = one_hot(256, offset_order)
        acc[...] = jnp.zeros_like(acc)

    width = k_ref.shape[1]
    grad_first = from_slabs(perm[...], gf_ref[...].reshape(512, width))
    product = times(k_ref[...], v_ref[...])
    for k in range(4):
        acc[k] += dot(grad_first[k], product[k * 128 : k * 128 + 128], cb=1)
    left = by_offset(sort[...], gm_ref[...].reshape(512, width))
    right = by_offset(sort[...], f_ref[...].reshape(512, width))
    for j in range(4):
        acc[4 + j] += dot(left[j], right[j], cb=1)

    @pl.when(pl.program_id(0) == pl.num_programs(0) - 1)
    def _():
        for j in range(4):
            acc[4 + j] = acc[4 + j] * pat_ref[...]
        core = core_ref[0]
        for z in range(4):
            keep_ref[z] = acc[:, pl.ds(pl.multiple_of(z * 32 + core * 16, 16), 16), :]
            send_ref[z] = acc[:, pl.ds(pl.multiple_of(z * 32 + 16 - core * 16, 16), 16), :]


def grads_kernel(blocks, gf_ref, k_ref, v_ref, gk_ref, gv_ref, perm):
    @pl.when(pl.program_id(0) == 0)
    def _():
        perm[...] = one_hot(256, slab_order)

    grad_first = from_slabs(perm[...], gf_ref[...].reshape(512, k_ref.shape[1]))
    for k in range(4):
        rows = slice(k * 128, k * 128 + 128)
        grad = dot(blocks[k], grad_first[k], ca=0)
        gk_ref[rows, :] = (grad * v_ref[rows, :].astype(F32)).astype(BF16)
        gv_ref[rows, :] = (grad * k_ref[rows, :].astype(F32)).astype(BF16)


def pair_kernel(z_ref, keep_ref, got_ref, own_ref, *out_refs):
    z = z_ref[0]
    own_ref[...] = keep_ref[z] + got_ref[z]
    for r, out in enumerate(out_refs, start=1):
        t = lax.rem(z + r, 4)
        out[...] = (keep_ref[t] + got_ref[t]).astype(BF16)


def on_device(query, key, value, block_weights, mix_weights, block_index, cotangent):
    channels = query.shape[2]
    q, k, v, cot = (a.reshape(512, channels) for a in (query, key, value, cotangent))
    width = WIDE
    grid = (channels // width,)
    rows, slab = rows_spec(width), slab_spec(width)
    smem = pl.BlockSpec(memory_space=pltpu.SMEM)
    row_shape = jax.ShapeDtypeStruct((512, channels), BF16)
    pinned_rows = pltpu.HBM((512, channels), BF16)
    slab_shape = pltpu.HBM((32, 16, channels), BF16)
    pair_shape = pltpu.HBM((32, 32, channels), BF16)
    perm = pltpu.VMEM((256, 256), BF16)
    size = 512 * channels * 2
    work = 2 * 512 * 512 * channels

    def exchange(x):
        return lax.all_to_all(x, "seq", split_axis=0, concat_axis=0, tiled=True)

    place = lax.axis_index("dp").astype(jnp.int32).reshape(1)
    core, z = place & 1, place >> 1

    def hop(r):
        return [(i, ((i // 2 + r) % 4) * 2 + i % 2) for i in range(8)]

    mate = [(i, i ^ 1) for i in range(8)]
    own_rows = pack("weights", block_weights, mix_weights)
    column = [own_rows] + [lax.ppermute(own_rows, "dp", hop(r)) for r in (1, 2, 3)]
    (gated,) = streamed(
        gate_body, "gate", [pinned(q), pinned(cot)], [slab_shape], STEP, scratch=[perm], prepare=make_slab_order,
        flops=work // 2, nbytes=3 * size,
    )
    gated, *column = lax.optimization_barrier((gated, *column))
    grad_cols = exchange(gated)
    other = lax.ppermute(jnp.stack(column), "dp", mate)
    shard_spec = whole(8, 16, 128)
    blocks, factor, factor_t, pattern = call(
        factor_kernel, "factor", (), [smem] + [shard_spec] * 4 + [whole(4, 8, 16, 128), whole(128, 16)],
        [VMEM_SPEC] * 4,
        [pltpu.VMEM((4, 128, 128), BF16), pltpu.VMEM((512, 512), BF16), pltpu.VMEM((512, 512), BF16),
         pltpu.VMEM((128, 128), F32)],
        [pltpu.VMEM((512, 512), BF16), pltpu.VMEM((4, 128, 128), BF16)], work, size,
    )(place, *column, other, block_index)
    out = call(first_kernel, "first", grid, [VMEM_SPEC, rows, rows], slab, pair_shape, [perm], work, 3 * size)(
        held(blocks), pinned(k), pinned(v)
    )
    out, grad_cols = streamed(
        factor_body, "back", [], [pair_shape], STEP, consts=[factor_t], resident=grad_cols, echo=slab_shape, out_rows=16, extra=[out],
        aliases={2: 0}, flops=work, nbytes=2 * size,
    )
    got = exchange(out)
    (mixed_cols,) = streamed(
        factor_body, "mix", [], [slab_shape], STEP, consts=[factor], resident=got,
        flops=work, nbytes=2 * size,
    )
    returned = exchange(mixed_cols)

    part = jax.ShapeDtypeStruct((4, 8, 16, 128), F32)
    send, keep = call(
        sums_kernel, "sums", grid,
        [smem, VMEM_SPEC, slab, slab, slab_spec(width, 1), rows, rows],
        [whole(4, 8, 16, 128), whole(4, 8, 16, 128)], [part, part],
        [perm, perm, pltpu.VMEM((8, 128, 128), F32)], 3 * work, 5 * size,
    )(core, held(pattern), grad_cols, got, got, pinned(k), pinned(v))
    grad_key, grad_value = call(
        grads_kernel, "grads", grid, [VMEM_SPEC, slab_spec(width, 1), rows, rows], [rows, rows],
        [row_shape, row_shape], [perm], work, 5 * size,
    )(held(blocks), got, pinned(k), pinned(v))
    swapped = lax.ppermute(send, "dp", mate)
    shard = jax.ShapeDtypeStruct((8, 16, 128), BF16)
    own, *others = call(
        pair_kernel, "pair", (), [smem, whole(4, 8, 16, 128), whole(4, 8, 16, 128)], [whole(8, 16, 128)] * 4,
        [jax.ShapeDtypeStruct((8, 16, 128), F32), shard, shard, shard],
    )(z, keep, swapped)
    total = own
    for r, other in enumerate(others, start=1):
        total = total + lax.ppermute(other, "dp", hop(r)).astype(F32)

    output, grad_query = streamed(
        tail_body, "tail", [returned, pinned(q), pinned(cot)], [pinned_rows, pinned_rows], STEP,
        scratch=[perm], prepare=make_slab_order, flops=work // 2, nbytes=5 * size,
    )
    wide = query.shape
    return (
        output.reshape(wide), grad_query.reshape(wide), grad_key.reshape(wide), grad_value.reshape(wide),
        total[0:4], total[4:8],
    )


def solution(mesh):
    placed = (
        P("dp", "seq", None),
        P("dp", "seq", None),
        P("dp", "seq", None),
        P("seq", "dp", None),
        P("seq", "dp", None),
        P(),
        P("dp", "seq", None),
    )
    return jax.shard_map(
        on_device,
        mesh=mesh,
        in_specs=placed,
        out_specs=(
            P("dp", "seq", None),
            P("dp", "seq", None),
            P("dp", "seq", None),
            P("dp", "seq", None),
            P("seq", "dp", None),
            P("seq", "dp", None),
        ),
        check_vma=False,
    )
```

```python
import jax
import jax.numpy as jnp
from jax import lax
from jax.experimental import pallas as pl
from jax.experimental.pallas import tpu as pltpu
from jax.sharding import PartitionSpec as P

BF16 = jnp.bfloat16
F32 = jnp.float32
MIB = 1024 * 1024
STEP = 512
WIDE = 512


def dot(a, b, ca=1, cb=0):
    return lax.dot_general(a, b, (((ca,), (cb,)), ((), ())), preferred_element_type=F32)


def one_hot(size, column_of):
    rows = lax.broadcasted_iota(jnp.int32, (size, size), 0)
    columns = lax.broadcasted_iota(jnp.int32, (size, size), 1)
    return (columns == column_of(rows)).astype(F32).astype(BF16)


def slab_order(r):
    return ((r >> 2) & 3) * 64 + (r >> 4) * 4 + (r & 3)


def offset_order(r):
    return (r & 63) * 4 + (r >> 6)


def to_slabs(perm, x):
    halves = []
    for g in range(2):
        part = jnp.concatenate([x[k * 128 + g * 64 : k * 128 + g * 64 + 64] for k in range(4)], axis=0)
        halves.append(dot(perm, part).astype(BF16))
    return jnp.concatenate(halves, axis=0)


def from_slabs(perm, x):
    halves = [dot(perm, x[g * 256 : g * 256 + 256], ca=0).astype(BF16) for g in range(2)]
    return [jnp.concatenate([h[k * 64 : k * 64 + 64] for h in halves], axis=0) for k in range(4)]


def by_offset(perm, x):
    halves = [dot(perm, x[g * 256 : g * 256 + 256]).astype(BF16) for g in range(2)]
    return [jnp.concatenate([h[j * 64 : j * 64 + 64] for h in halves], axis=0) for j in range(4)]


def times(a, b):
    return (a.astype(F32) * b.astype(F32)).astype(BF16)


def call(kernel, name, grid, in_specs, out_specs, out_shape, scratch=(), flops=0, nbytes=0, aliases=None, vmem=12):
    return pl.pallas_call(
        kernel,
        name=name,
        grid=grid,
        in_specs=in_specs,
        out_specs=out_specs,
        out_shape=out_shape,
        scratch_shapes=list(scratch),
        input_output_aliases=aliases or {},
        cost_estimate=pl.CostEstimate(flops=flops, transcendentals=0, bytes_accessed=nbytes),
        compiler_params=pltpu.CompilerParams(
            vmem_limit_bytes=vmem * MIB, dimension_semantics=("arbitrary",) * len(grid)
        ),
    )


def chunk_of(ref, index, width, rows=0):
    columns = pl.ds(index * width, width)
    if len(ref.shape) == 2:
        return ref.at[:, columns]
    return ref.at[:, pl.ds(rows, 16), columns] if ref.shape[0] == 32 else ref.at[:, :, columns]


def streamed(body, name, ins, out_shapes, width, consts=(), resident=None, out_rows=0, extra=(), aliases=None, scratch=(),
             prepare=None, echo=None, flops=0, nbytes=0, vmem=16):
    channels = out_shapes[0].shape[-1]
    count = channels // width
    vmem_in = list(consts) + ([] if resident is None else [resident])
    n_vmem, n_in, n_extra, n_out = len(vmem_in), len(ins), len(extra), len(out_shapes)

    def buffer(array):
        shape = array.shape
        return pltpu.VMEM((count, *((32, 16) if len(shape) == 3 and shape[0] == 32 else shape[:-1]), width), BF16)

    def kernel(*refs):
        vmem_refs, refs = refs[:n_vmem], refs[n_vmem:]
        in_refs, refs = refs[:n_in], refs[n_in + n_extra :]
        out_refs, refs = refs[:n_out], refs[n_out:]
        leaving = []
        if echo is not None:
            leaving.append(pltpu.make_async_copy(vmem_refs[-1], refs[0], refs[-1].at[0]))
            leaving[0].start()
            refs = refs[1:-1]
        bufs, refs = refs[:n_in], refs[n_in:]
        outs, refs = refs[:n_out], refs[n_out:]
        in_sem, out_sem, scratch_refs = refs[0], refs[1], refs[2:]
        arriving = []
        for c in range(count):
            arriving.append([
                pltpu.make_async_copy(chunk_of(in_refs[i], c, width), bufs[i].at[c], in_sem.at[i, c]) for i in range(n_in)
            ])
            for copy in arriving[c]:
                copy.start()
        if prepare is not None:
            prepare(*scratch_refs)
        for c in range(count):
            for copy in arriving[c]:
                copy.wait()
            values = [buf[c].reshape(512, width) for buf in bufs]
            if resident is not None:
                values = [vmem_refs[-1][:, 0:16, c * width : c * width + width].reshape(512, width)] + values
            for o, make in enumerate(body(vmem_refs, scratch_refs, *values)):
                outs[o][c] = make().reshape(outs[o].shape[1:])
                copy = pltpu.make_async_copy(outs[o].at[c], chunk_of(out_refs[o], c, width, out_rows), out_sem.at[o, c])
                copy.start()
                leaving.append(copy)
        for copy in leaving:
            copy.wait()

    return pl.pallas_call(
        kernel,
        name=name,
        in_specs=[VMEM_SPEC] * n_vmem + [pl.BlockSpec(memory_space=pl.ANY)] * (n_in + n_extra),
        out_specs=[pl.BlockSpec(memory_space=pltpu.HBM)] * (n_out + (echo is not None)),
        out_shape=list(out_shapes) + ([] if echo is None else [echo]),
        scratch_shapes=[buffer(x) for x in ins]
        + [buffer(x) for x in out_shapes]
        + [pltpu.SemaphoreType.DMA((max(n_in, 1), count)), pltpu.SemaphoreType.DMA((n_out, count))]
        + list(scratch)
        + ([] if echo is None else [pltpu.SemaphoreType.DMA((1,))]),
        input_output_aliases=aliases or {},
        cost_estimate=pl.CostEstimate(flops=flops, transcendentals=0, bytes_accessed=nbytes),
        compiler_params=pltpu.CompilerParams(vmem_limit_bytes=vmem * MIB),
    )(*[held(x) for x in vmem_in], *ins, *extra)


def pinned(x):
    return pltpu.with_memory_space_constraint(x, pltpu.HBM)


def held(x):
    return pltpu.with_memory_space_constraint(x, pltpu.VMEM)


def rows_spec(width):
    return pl.BlockSpec((512, width), lambda d: (0, d))


def slab_spec(width, half=0):
    return pl.BlockSpec((32, 16, width), lambda d: (0, half, d))


def whole(*shape):
    return pl.BlockSpec(shape, lambda *g: (0,) * len(shape))


VMEM_SPEC = pl.BlockSpec(memory_space=pltpu.VMEM)


def make_slab_order(perm):
    perm[...] = one_hot(256, slab_order)


def gate_body(consts, scratch, q, cot):
    return [lambda: to_slabs(scratch[0][...], times(q, cot))]


def factor_body(consts, scratch, x):
    return [lambda: dot(consts[0][...], x).astype(BF16)]


def tail_body(consts, scratch, x, q, cot):
    mixed = jnp.concatenate(from_slabs(scratch[0][...], x), axis=0)
    return [lambda: times(q, mixed), lambda: times(cot, mixed)]


def pack_kernel(*refs):
    ins, out_ref, sem = refs[:-2], refs[-2], refs[-1]
    copies, start = [], 0
    for i, ref in enumerate(ins):
        copies.append(pltpu.make_async_copy(ref, out_ref.at[pl.ds(start, ref.shape[0])], sem.at[i]))
        start += ref.shape[0]
    for copy in copies:
        copy.start()
    for copy in copies:
        copy.wait()


def pack(name, *arrays):
    shape = (sum(a.shape[0] for a in arrays), *arrays[0].shape[1:])
    return pl.pallas_call(
        pack_kernel,
        name=name,
        in_specs=[pl.BlockSpec(memory_space=pl.ANY)] * len(arrays),
        out_specs=VMEM_SPEC,
        out_shape=pltpu.VMEM(shape, arrays[0].dtype),
        scratch_shapes=[pltpu.SemaphoreType.DMA((len(arrays),))],
        compiler_params=pltpu.CompilerParams(vmem_limit_bytes=4 * MIB),
    )(*[pinned(a) for a in arrays])


def first_kernel(blocks, k_ref, v_ref, o_ref, perm):
    @pl.when(pl.program_id(0) == 0)
    def _():
        perm[...] = one_hot(256, slab_order)

    product = times(k_ref[...], v_ref[...])
    first = jnp.concatenate(
        [dot(blocks[k], product[k * 128 : k * 128 + 128]).astype(BF16) for k in range(4)], axis=0
    )
    o_ref[...] = to_slabs(perm[...], first).reshape(o_ref.shape)


def factor_kernel(place_ref, w0_ref, w1_ref, w2_ref, w3_ref, mate_ref, idx_ref, b_ref, m_ref, mt_ref, p_ref, diag, mixes):
    place = place_ref[0]
    core = lax.rem(place, 2)
    for r, w_ref in enumerate((w0_ref, w1_ref, w2_ref, w3_ref)):
        z = lax.rem(lax.div(place, 2) + 4 - r, 4)
        own = pl.ds(pl.multiple_of(z * 32 + core * 16, 16), 16)
        mate = pl.ds(pl.multiple_of(z * 32 + 16 - core * 16, 16), 16)
        b_ref[:, own, :] = w_ref[0:4]
        b_ref[:, mate, :] = mate_ref[r, 0:4]
        mixes[:, own, :] = w_ref[4:8]
        mixes[:, mate, :] = mate_ref[r, 4:8]
    columns = lax.broadcasted_iota(jnp.int32, (128, 128), 1)
    hits = jnp.zeros((128, 128), F32)
    for n in range(idx_ref.shape[1]):
        hits = jnp.maximum(hits, (idx_ref[:, n : n + 1] == columns).astype(F32))
    p_ref[...] = hits
    diag[...] = jnp.zeros_like(diag)
    for j in range(4):
        diag[j * 128 : j * 128 + 128, j * 128 : j * 128 + 128] = (mixes[j].astype(F32) * hits).astype(BF16)
    spread = one_hot(512, lambda r: (r & 3) * 128 + (r >> 2))
    rows = dot(spread, diag[...]).astype(BF16)
    m_ref[...] = dot(rows, spread, cb=1).astype(BF16)
    rows_t = dot(spread, diag[...], cb=1).astype(BF16)
    mt_ref[...] = dot(rows_t, spread, cb=1).astype(BF16)


def sums_kernel(core_ref, pat_ref, gm_ref, f_ref, gf_ref, k_ref, v_ref, send_ref, keep_ref, perm, sort, acc):
    @pl.when(pl.program_id(0) == 0)
    def _():
        perm[...] = one_hot(256, slab_order)
        sort[...] = one_hot(256, offset_order)
        acc[...] = jnp.zeros_like(acc)

    width = k_ref.shape[1]
    grad_first = from_slabs(perm[...], gf_ref[...].reshape(512, width))
    product = times(k_ref[...], v_ref[...])
    for k in range(4):
        acc[k] += dot(grad_first[k], product[k * 128 : k * 128 + 128], cb=1)
    left = by_offset(sort[...], gm_ref[...].reshape(512, width))
    right = by_offset(sort[...], f_ref[...].reshape(512, width))
    for j in range(4):
        acc[4 + j] += dot(left[j], right[j], cb=1)

    @pl.when(pl.program_id(0) == pl.num_programs(0) - 1)
    def _():
        for j in range(4):
            acc[4 + j] = acc[4 + j] * pat_ref[...]
        core = core_ref[0]
        for z in range(4):
            keep_ref[z] = acc[:, pl.ds(pl.multiple_of(z * 32 + core * 16, 16), 16), :]
            send_ref[z] = acc[:, pl.ds(pl.multiple_of(z * 32 + 16 - core * 16, 16), 16), :]


def grads_kernel(blocks, gf_ref, k_ref, v_ref, gk_ref, gv_ref, perm):
    @pl.when(pl.program_id(0) == 0)
    def _():
        perm[...] = one_hot(256, slab_order)

    grad_first = from_slabs(perm[...], gf_ref[...].reshape(512, k_ref.shape[1]))
    for k in range(4):
        rows = slice(k * 128, k * 128 + 128)
        grad = dot(blocks[k], grad_first[k], ca=0)
        gk_ref[rows, :] = (grad * v_ref[rows, :].astype(F32)).astype(BF16)
        gv_ref[rows, :] = (grad * k_ref[rows, :].astype(F32)).astype(BF16)


def pair_kernel(z_ref, keep_ref, got_ref, own_ref, *out_refs):
    z = z_ref[0]
    own_ref[...] = keep_ref[z] + got_ref[z]
    for r, out in enumerate(out_refs, start=1):
        t = lax.rem(z + r, 4)
        out[...] = (keep_ref[t] + got_ref[t]).astype(BF16)


def on_device(query, key, value, block_weights, mix_weights, block_index, cotangent):
    channels = query.shape[2]
    q, k, v, cot = (a.reshape(512, channels) for a in (query, key, value, cotangent))
    width = WIDE
    grid = (channels // width,)
    rows, slab = rows_spec(width), slab_spec(width)
    smem = pl.BlockSpec(memory_space=pltpu.SMEM)
    row_shape = jax.ShapeDtypeStruct((512, channels), BF16)
    pinned_rows = pltpu.HBM((512, channels), BF16)
    slab_shape = pltpu.HBM((32, 16, channels), BF16)
    pair_shape = pltpu.HBM((32, 32, channels), BF16)
    perm = pltpu.VMEM((256, 256), BF16)
    size = 512 * channels * 2
    work = 2 * 512 * 512 * channels

    def exchange(x):
        return lax.all_to_all(x, "seq", split_axis=0, concat_axis=0, tiled=True)

    place = lax.axis_index("dp").astype(jnp.int32).reshape(1)
    core, z = place & 1, place >> 1

    def hop(r):
        return [(i, ((i // 2 + r) % 4) * 2 + i % 2) for i in range(8)]

    mate = [(i, i ^ 1) for i in range(8)]
    own_rows = pack("weights", block_weights, mix_weights)
    column = [own_rows] + [lax.ppermute(own_rows, "dp", hop(r)) for r in (1, 2, 3)]
    (gated,) = streamed(
        gate_body, "gate", [pinned(q), pinned(cot)], [slab_shape], STEP, scratch=[perm], prepare=make_slab_order,
        flops=work // 2, nbytes=3 * size,
    )
    grad_cols = exchange(gated)
    other = lax.ppermute(jnp.stack(column), "dp", mate)
    shard_spec = whole(8, 16, 128)
    blocks, factor, factor_t, pattern = call(
        factor_kernel, "factor", (), [smem] + [shard_spec] * 4 + [whole(4, 8, 16, 128), whole(128, 16)],
        [VMEM_SPEC] * 4,
        [pltpu.VMEM((4, 128, 128), BF16), pltpu.VMEM((512, 512), BF16), pltpu.VMEM((512, 512), BF16),
         pltpu.VMEM((128, 128), F32)],
        [pltpu.VMEM((512, 512), BF16), pltpu.VMEM((4, 128, 128), BF16)], work, size,
    )(place, *column, other, block_index)
    out = call(first_kernel, "first", grid, [VMEM_SPEC, rows, rows], slab, pair_shape, [perm], 36 * work, 3 * size)(
        held(blocks), pinned(k), pinned(v)
    )
    out, grad_cols = streamed(
        factor_body, "back", [], [pair_shape], STEP, consts=[factor_t], resident=grad_cols, echo=slab_shape, out_rows=16, extra=[out],
        aliases={2: 0}, flops=work, nbytes=2 * size,
    )
    got = exchange(out)
    (mixed_cols,) = streamed(
        factor_body, "mix", [], [slab_shape], STEP, consts=[factor], resident=got,
        flops=work, nbytes=2 * size,
    )
    returned = exchange(mixed_cols)

    part = jax.ShapeDtypeStruct((4, 8, 16, 128), F32)
    send, keep = call(
        sums_kernel, "sums", grid,
        [smem, VMEM_SPEC, slab, slab, slab_spec(width, 1), rows, rows],
        [whole(4, 8, 16, 128), whole(4, 8, 16, 128)], [part, part],
        [perm, perm, pltpu.VMEM((8, 128, 128), F32)], 3 * work, 5 * size,
    )(core, held(pattern), pinned(grad_cols), got, got, pinned(k), pinned(v))
    grad_key, grad_value = call(
        grads_kernel, "grads", grid, [VMEM_SPEC, slab_spec(width, 1), rows, rows], [rows, rows],
        [row_shape, row_shape], [perm], work, 5 * size,
    )(held(blocks), got, pinned(k), pinned(v))
    swapped = lax.ppermute(send, "dp", mate)
    shard = jax.ShapeDtypeStruct((8, 16, 128), BF16)
    own, *others = call(
        pair_kernel, "pair", (), [smem, whole(4, 8, 16, 128), whole(4, 8, 16, 128)], [whole(8, 16, 128)] * 4,
        [jax.ShapeDtypeStruct((8, 16, 128), F32), shard, shard, shard],
    )(z, keep, swapped)
    total = own
    for r, other in enumerate(others, start=1):
        total = total + lax.ppermute(other, "dp", hop(r)).astype(F32)

    output, grad_query = streamed(
        tail_body, "tail", [returned, pinned(q), pinned(cot)], [pinned_rows, pinned_rows], STEP,
        scratch=[perm], prepare=make_slab_order, flops=work // 2, nbytes=5 * size,
    )
    wide = query.shape
    return (
        output.reshape(wide), grad_query.reshape(wide), grad_key.reshape(wide), grad_value.reshape(wide),
        total[0:4], total[4:8],
    )


def solution(mesh):
    placed = (
        P("dp", "seq", None),
        P("dp", "seq", None),
        P("dp", "seq", None),
        P("seq", "dp", None),
        P("seq", "dp", None),
        P(),
        P("dp", "seq", None),
    )
    return jax.shard_map(
        on_device,
        mesh=mesh,
        in_specs=placed,
        out_specs=(
            P("dp", "seq", None),
            P("dp", "seq", None),
            P("dp", "seq", None),
            P("dp", "seq", None),
            P("seq", "dp", None),
            P("seq", "dp", None),
        ),
        check_vma=False,
    )
```

```python
import jax
import jax.numpy as jnp
from jax import lax
from jax.experimental import pallas as pl
from jax.experimental.pallas import tpu as pltpu
from jax.sharding import PartitionSpec as P

BF16 = jnp.bfloat16
F32 = jnp.float32
MIB = 1024 * 1024
STEP = 512
BROAD = 768
WIDE = 512


def dot(a, b, ca=1, cb=0):
    return lax.dot_general(a, b, (((ca,), (cb,)), ((), ())), preferred_element_type=F32)


def one_hot(size, column_of):
    rows = lax.broadcasted_iota(jnp.int32, (size, size), 0)
    columns = lax.broadcasted_iota(jnp.int32, (size, size), 1)
    return (columns == column_of(rows)).astype(F32).astype(BF16)


def slab_order(r):
    return ((r >> 2) & 3) * 64 + (r >> 4) * 4 + (r & 3)


def offset_order(r):
    return (r & 63) * 4 + (r >> 6)


def to_slabs(perm, x):
    halves = []
    for g in range(2):
        part = jnp.concatenate([x[k * 128 + g * 64 : k * 128 + g * 64 + 64] for k in range(4)], axis=0)
        halves.append(dot(perm, part).astype(BF16))
    return jnp.concatenate(halves, axis=0)


def from_slabs(perm, x):
    halves = [dot(perm, x[g * 256 : g * 256 + 256], ca=0).astype(BF16) for g in range(2)]
    return [jnp.concatenate([h[k * 64 : k * 64 + 64] for h in halves], axis=0) for k in range(4)]


def by_offset(perm, x):
    halves = [dot(perm, x[g * 256 : g * 256 + 256]).astype(BF16) for g in range(2)]
    return [jnp.concatenate([h[j * 64 : j * 64 + 64] for h in halves], axis=0) for j in range(4)]


def times(a, b):
    return (a.astype(F32) * b.astype(F32)).astype(BF16)


def call(kernel, name, grid, in_specs, out_specs, out_shape, scratch=(), flops=0, nbytes=0, aliases=None, vmem=12):
    return pl.pallas_call(
        kernel,
        name=name,
        grid=grid,
        in_specs=in_specs,
        out_specs=out_specs,
        out_shape=out_shape,
        scratch_shapes=list(scratch),
        input_output_aliases=aliases or {},
        cost_estimate=pl.CostEstimate(flops=flops, transcendentals=0, bytes_accessed=nbytes),
        compiler_params=pltpu.CompilerParams(
            vmem_limit_bytes=vmem * MIB, dimension_semantics=("arbitrary",) * len(grid)
        ),
    )


def chunk_of(ref, index, width, rows=0):
    columns = pl.ds(index * width, width)
    if len(ref.shape) == 2:
        return ref.at[:, columns]
    return ref.at[:, pl.ds(rows, 16), columns] if ref.shape[0] == 32 else ref.at[:, :, columns]


def streamed(body, name, ins, out_shapes, width, consts=(), resident=None, out_rows=0, extra=(), aliases=None, scratch=(),
             prepare=None, echo=None, flops=0, nbytes=0, vmem=16):
    channels = out_shapes[0].shape[-1]
    count = channels // width
    vmem_in = list(consts) + ([] if resident is None else [resident])
    n_vmem, n_in, n_extra, n_out = len(vmem_in), len(ins), len(extra), len(out_shapes)

    def buffer(array):
        shape = array.shape
        return pltpu.VMEM((count, *((32, 16) if len(shape) == 3 and shape[0] == 32 else shape[:-1]), width), BF16)

    def kernel(*refs):
        vmem_refs, refs = refs[:n_vmem], refs[n_vmem:]
        in_refs, refs = refs[:n_in], refs[n_in + n_extra :]
        out_refs, refs = refs[:n_out], refs[n_out:]
        leaving = []
        if echo is not None:
            leaving.append(pltpu.make_async_copy(vmem_refs[-1], refs[0], refs[-1].at[0]))
            leaving[0].start()
            refs = refs[1:-1]
        bufs, refs = refs[:n_in], refs[n_in:]
        outs, refs = refs[:n_out], refs[n_out:]
        in_sem, out_sem, scratch_refs = refs[0], refs[1], refs[2:]
        arriving = []
        for c in range(count):
            arriving.append([
                pltpu.make_async_copy(chunk_of(in_refs[i], c, width), bufs[i].at[c], in_sem.at[i, c]) for i in range(n_in)
            ])
            for copy in arriving[c]:
                copy.start()
        if prepare is not None:
            prepare(*scratch_refs)
        for c in range(count):
            for copy in arriving[c]:
                copy.wait()
            values = [buf[c].reshape(512, width) for buf in bufs]
            if resident is not None:
                values = [vmem_refs[-1][:, 0:16, c * width : c * width + width].reshape(512, width)] + values
            for o, make in enumerate(body(vmem_refs, scratch_refs, *values)):
                outs[o][c] = make().reshape(outs[o].shape[1:])
                copy = pltpu.make_async_copy(outs[o].at[c], chunk_of(out_refs[o], c, width, out_rows), out_sem.at[o, c])
                copy.start()
                leaving.append(copy)
        for copy in leaving:
            copy.wait()

    return pl.pallas_call(
        kernel,
        name=name,
        in_specs=[VMEM_SPEC] * n_vmem + [pl.BlockSpec(memory_space=pl.ANY)] * (n_in + n_extra),
        out_specs=[pl.BlockSpec(memory_space=pltpu.HBM)] * (n_out + (echo is not None)),
        out_shape=list(out_shapes) + ([] if echo is None else [echo]),
        scratch_shapes=[buffer(x) for x in ins]
        + [buffer(x) for x in out_shapes]
        + [pltpu.SemaphoreType.DMA((max(n_in, 1), count)), pltpu.SemaphoreType.DMA((n_out, count))]
        + list(scratch)
        + ([] if echo is None else [pltpu.SemaphoreType.DMA((1,))]),
        input_output_aliases=aliases or {},
        cost_estimate=pl.CostEstimate(flops=flops, transcendentals=0, bytes_accessed=nbytes),
        compiler_params=pltpu.CompilerParams(vmem_limit_bytes=vmem * MIB),
    )(*[held(x) for x in vmem_in], *ins, *extra)


def pinned(x):
    return pltpu.with_memory_space_constraint(x, pltpu.HBM)


def held(x):
    return pltpu.with_memory_space_constraint(x, pltpu.VMEM)


def rows_spec(width):
    return pl.BlockSpec((512, width), lambda d: (0, d))


def slab_spec(width, half=0):
    return pl.BlockSpec((32, 16, width), lambda d: (0, half, d))


def whole(*shape):
    return pl.BlockSpec(shape, lambda *g: (0,) * len(shape))


VMEM_SPEC = pl.BlockSpec(memory_space=pltpu.VMEM)


def make_slab_order(perm):
    perm[...] = one_hot(256, slab_order)


def gate_body(consts, scratch, q, cot):
    return [lambda: to_slabs(scratch[0][...], times(q, cot))]


def factor_body(consts, scratch, x):
    return [lambda: dot(consts[0][...], x).astype(BF16)]


def tail_body(consts, scratch, x, q, cot):
    mixed = jnp.concatenate(from_slabs(scratch[0][...], x), axis=0)
    return [lambda: times(q, mixed), lambda: times(cot, mixed)]


def pack_kernel(*refs):
    ins, out_ref, sem = refs[:-2], refs[-2], refs[-1]
    copies, start = [], 0
    for i, ref in enumerate(ins):
        copies.append(pltpu.make_async_copy(ref, out_ref.at[pl.ds(start, ref.shape[0])], sem.at[i]))
        start += ref.shape[0]
    for copy in copies:
        copy.start()
    for copy in copies:
        copy.wait()


def pack(name, *arrays):
    shape = (sum(a.shape[0] for a in arrays), *arrays[0].shape[1:])
    return pl.pallas_call(
        pack_kernel,
        name=name,
        in_specs=[pl.BlockSpec(memory_space=pl.ANY)] * len(arrays),
        out_specs=VMEM_SPEC,
        out_shape=pltpu.VMEM(shape, arrays[0].dtype),
        scratch_shapes=[pltpu.SemaphoreType.DMA((len(arrays),))],
        compiler_params=pltpu.CompilerParams(vmem_limit_bytes=4 * MIB),
    )(*[pinned(a) for a in arrays])


def first_kernel(blocks, k_ref, v_ref, o_ref, perm):
    @pl.when(pl.program_id(0) == 0)
    def _():
        perm[...] = one_hot(256, slab_order)

    product = times(k_ref[...], v_ref[...])
    first = jnp.concatenate(
        [dot(blocks[k], product[k * 128 : k * 128 + 128]).astype(BF16) for k in range(4)], axis=0
    )
    o_ref[...] = to_slabs(perm[...], first).reshape(o_ref.shape)


def factor_kernel(place_ref, w0_ref, w1_ref, w2_ref, w3_ref, mate_ref, idx_ref, b_ref, m_ref, mt_ref, p_ref, diag, mixes):
    place = place_ref[0]
    core = lax.rem(place, 2)
    for r, w_ref in enumerate((w0_ref, w1_ref, w2_ref, w3_ref)):
        z = lax.rem(lax.div(place, 2) + 4 - r, 4)
        own = pl.ds(pl.multiple_of(z * 32 + core * 16, 16), 16)
        mate = pl.ds(pl.multiple_of(z * 32 + 16 - core * 16, 16), 16)
        b_ref[:, own, :] = w_ref[0:4]
        b_ref[:, mate, :] = mate_ref[r, 0:4]
        mixes[:, own, :] = w_ref[4:8]
        mixes[:, mate, :] = mate_ref[r, 4:8]
    columns = lax.broadcasted_iota(jnp.int32, (128, 128), 1)
    hits = jnp.zeros((128, 128), F32)
    for n in range(idx_ref.shape[1]):
        hits = jnp.maximum(hits, (idx_ref[:, n : n + 1] == columns).astype(F32))
    p_ref[...] = hits
    diag[...] = jnp.zeros_like(diag)
    for j in range(4):
        diag[j * 128 : j * 128 + 128, j * 128 : j * 128 + 128] = (mixes[j].astype(F32) * hits).astype(BF16)
    spread = one_hot(512, lambda r: (r & 3) * 128 + (r >> 2))
    rows = dot(spread, diag[...]).astype(BF16)
    m_ref[...] = dot(rows, spread, cb=1).astype(BF16)
    rows_t = dot(spread, diag[...], cb=1).astype(BF16)
    mt_ref[...] = dot(rows_t, spread, cb=1).astype(BF16)


def sums_kernel(core_ref, pat_ref, gm_ref, f_ref, gf_ref, k_ref, v_ref, send_ref, keep_ref, perm, sort, acc):
    @pl.when(pl.program_id(0) == 0)
    def _():
        perm[...] = one_hot(256, slab_order)
        sort[...] = one_hot(256, offset_order)
        acc[...] = jnp.zeros_like(acc)

    width = k_ref.shape[1]
    grad_first = from_slabs(perm[...], gf_ref[...].reshape(512, width))
    product = times(k_ref[...], v_ref[...])
    for k in range(4):
        acc[k] += dot(grad_first[k], product[k * 128 : k * 128 + 128], cb=1)
    left = by_offset(sort[...], gm_ref[...].reshape(512, width))
    right = by_offset(sort[...], f_ref[...].reshape(512, width))
    for j in range(4):
        acc[4 + j] += dot(left[j], right[j], cb=1)

    @pl.when(pl.program_id(0) == pl.num_programs(0) - 1)
    def _():
        for j in range(4):
            acc[4 + j] = acc[4 + j] * pat_ref[...]
        core = core_ref[0]
        for z in range(4):
            keep_ref[z] = acc[:, pl.ds(pl.multiple_of(z * 32 + core * 16, 16), 16), :]
            send_ref[z] = acc[:, pl.ds(pl.multiple_of(z * 32 + 16 - core * 16, 16), 16), :]


def grads_kernel(blocks, gf_ref, k_ref, v_ref, gk_ref, gv_ref, perm):
    @pl.when(pl.program_id(0) == 0)
    def _():
        perm[...] = one_hot(256, slab_order)

    grad_first = from_slabs(perm[...], gf_ref[...].reshape(512, k_ref.shape[1]))
    for k in range(4):
        rows = slice(k * 128, k * 128 + 128)
        grad = dot(blocks[k], grad_first[k], ca=0)
        gk_ref[rows, :] = (grad * v_ref[rows, :].astype(F32)).astype(BF16)
        gv_ref[rows, :] = (grad * k_ref[rows, :].astype(F32)).astype(BF16)


def pair_kernel(z_ref, keep_ref, got_ref, own_ref, *out_refs):
    z = z_ref[0]
    own_ref[...] = keep_ref[z] + got_ref[z]
    for r, out in enumerate(out_refs, start=1):
        t = lax.rem(z + r, 4)
        out[...] = (keep_ref[t] + got_ref[t]).astype(BF16)


def on_device(query, key, value, block_weights, mix_weights, block_index, cotangent):
    channels = query.shape[2]
    q, k, v, cot = (a.reshape(512, channels) for a in (query, key, value, cotangent))
    width = WIDE
    grid = (channels // width,)
    rows, slab = rows_spec(width), slab_spec(width)
    smem = pl.BlockSpec(memory_space=pltpu.SMEM)
    row_shape = jax.ShapeDtypeStruct((512, channels), BF16)
    pinned_rows = pltpu.HBM((512, channels), BF16)
    slab_shape = pltpu.HBM((32, 16, channels), BF16)
    pair_shape = pltpu.HBM((32, 32, channels), BF16)
    perm = pltpu.VMEM((256, 256), BF16)
    size = 512 * channels * 2
    work = 2 * 512 * 512 * channels

    def exchange(x):
        return lax.all_to_all(x, "seq", split_axis=0, concat_axis=0, tiled=True)

    place = lax.axis_index("dp").astype(jnp.int32).reshape(1)
    core, z = place & 1, place >> 1

    def hop(r):
        return [(i, ((i // 2 + r) % 4) * 2 + i % 2) for i in range(8)]

    mate = [(i, i ^ 1) for i in range(8)]
    own_rows = pack("weights", block_weights, mix_weights)
    column = [own_rows] + [lax.ppermute(own_rows, "dp", hop(r)) for r in (1, 2, 3)]
    (gated,) = streamed(
        gate_body, "gate", [pinned(q), pinned(cot)], [slab_shape], BROAD, scratch=[perm], prepare=make_slab_order,
        flops=work // 2, nbytes=3 * size,
    )
    gated, *column = lax.optimization_barrier((gated, *column))
    grad_cols = exchange(gated)
    other = lax.ppermute(jnp.stack(column), "dp", mate)
    shard_spec = whole(8, 16, 128)
    blocks, factor, factor_t, pattern = call(
        factor_kernel, "factor", (), [smem] + [shard_spec] * 4 + [whole(4, 8, 16, 128), whole(128, 16)],
        [VMEM_SPEC] * 4,
        [pltpu.VMEM((4, 128, 128), BF16), pltpu.VMEM((512, 512), BF16), pltpu.VMEM((512, 512), BF16),
         pltpu.VMEM((128, 128), F32)],
        [pltpu.VMEM((512, 512), BF16), pltpu.VMEM((4, 128, 128), BF16)], work, size,
    )(place, *column, other, block_index)
    out = call(first_kernel, "first", grid, [VMEM_SPEC, rows, rows], slab, pair_shape, [perm], work, 3 * size)(
        held(blocks), pinned(k), pinned(v)
    )
    out, grad_cols = streamed(
        factor_body, "back", [], [pair_shape], STEP, consts=[factor_t], resident=grad_cols, echo=slab_shape, out_rows=16, extra=[out],
        aliases={2: 0}, flops=work, nbytes=2 * size,
    )
    got = exchange(out)
    (mixed_cols,) = streamed(
        factor_body, "mix", [], [slab_shape], STEP, consts=[factor], resident=got,
        flops=work, nbytes=2 * size,
    )
    returned = exchange(mixed_cols)

    part = jax.ShapeDtypeStruct((4, 8, 16, 128), F32)
    send, keep = call(
        sums_kernel, "sums", grid,
        [smem, VMEM_SPEC, slab, slab, slab_spec(width, 1), rows, rows],
        [whole(4, 8, 16, 128), whole(4, 8, 16, 128)], [part, part],
        [perm, perm, pltpu.VMEM((8, 128, 128), F32)], 3 * work, 5 * size,
    )(core, held(pattern), pinned(grad_cols), got, got, pinned(k), pinned(v))
    grad_key, grad_value = call(
        grads_kernel, "grads", grid, [VMEM_SPEC, slab_spec(width, 1), rows, rows], [rows, rows],
        [row_shape, row_shape], [perm], work, 5 * size,
    )(held(blocks), got, pinned(k), pinned(v))
    swapped = lax.ppermute(send, "dp", mate)
    shard = jax.ShapeDtypeStruct((8, 16, 128), BF16)
    own, *others = call(
        pair_kernel, "pair", (), [smem, whole(4, 8, 16, 128), whole(4, 8, 16, 128)], [whole(8, 16, 128)] * 4,
        [jax.ShapeDtypeStruct((8, 16, 128), F32), shard, shard, shard],
    )(z, keep, swapped)
    total = own
    for r, other in enumerate(others, start=1):
        total = total + lax.ppermute(other, "dp", hop(r)).astype(F32)

    output, grad_query = streamed(
        tail_body, "tail", [returned, pinned(q), pinned(cot)], [pinned_rows, pinned_rows], BROAD,
        scratch=[perm], prepare=make_slab_order, flops=work // 2, nbytes=5 * size,
    )
    wide = query.shape
    return (
        output.reshape(wide), grad_query.reshape(wide), grad_key.reshape(wide), grad_value.reshape(wide),
        total[0:4], total[4:8],
    )


def solution(mesh):
    placed = (
        P("dp", "seq", None),
        P("dp", "seq", None),
        P("dp", "seq", None),
        P("seq", "dp", None),
        P("seq", "dp", None),
        P(),
        P("dp", "seq", None),
    )
    return jax.shard_map(
        on_device,
        mesh=mesh,
        in_specs=placed,
        out_specs=(
            P("dp", "seq", None),
            P("dp", "seq", None),
            P("dp", "seq", None),
            P("dp", "seq", None),
            P("seq", "dp", None),
            P("seq", "dp", None),
        ),
        check_vma=False,
    )
```
